32 devices in a mesh: gx: 8 (over z, y), gy: 4 (over x, core).
Axes of the slice: x: 2, y: 2, z: 4, core: 2. Of those that a mesh axis runs over, the one named last changes fastest.
Arguments:
- conc_start: float32 [64, 32, 128], P('gx', 'gy'), may hold values from 0.5 to 2
- diffusion: float32 [64, 32, 128], P('gx', 'gy'), may hold values from 0.03 to 0.12
- courant: float32 [64, 32, 128], P('gx', 'gy'), may hold values from 0.05 to 0.25
- uptake: float32 [64, 32, 128], P('gx', 'gy'), may hold values from 0.02 to 0.2
- directions: float32 [32, 64, 32, 128], P(None, 'gx', 'gy'), may hold values from -6 to 6
- sensor_cell: int32 [8, 4, 64], P('gx', 'gy'), may hold values from 0 to 8191
- sensor_step: int32 [8, 4, 64], P('gx', 'gy'), may hold values from 1 to 4
Outputs:
- curvature_product: float32 [32, 64, 32, 128], P(None, 'gx', 'gy')
The draws below stay inside these ranges and needn't reach their ends.
All inputs are finite; a program needn't handle non-finite values.
Results may differ from the reference program's by a relative error of at most 0.00002.
Values sent between devices are 32-bit elements; how exact they have to be, the bound alone decides.
A program may use at most 64 MiB of HBM per device.

```python
import math
import jax
import jax.numpy as jnp
from jax import lax

CX = 8
CY = 8
LZ = 128
NDIR = 32
STEPS = 4
S_DEV = 64
NX = 64
NY = 32
N_GX = 8
N_GY = 4


def with_ends(result, own_key, low, largest):
    spot = [jax.random.randint(jax.random.fold_in(own_key, axis), (), 0, length) for axis, length in enumerate(result.shape)]
    widest = result.shape.index(max(result.shape))
    neighbour = spot[:widest] + [(spot[widest] + 1) % result.shape[widest]] + spot[widest + 1:]
    return result.at[tuple(spot)].set(low).at[tuple(neighbour)].set(largest)


def block_levels(stream_key, extent, split, least, high):
    factor_of, own = 1.0, jax.random.fold_in(stream_key, 6)
    for dim, shards_of in split:
        steps = jnp.exp(jax.random.uniform(jax.random.fold_in(own, dim), (shards_of,), jnp.float32, least / len(split), high / len(split)))
        factor_of = factor_of * jnp.repeat(steps, extent[dim] // shards_of).reshape([-1 if axis == dim else 1 for axis in range(len(extent))])
    return factor_of


def centred(own_key, extent, scale, reach, pieces=(), kind=jnp.bfloat16):
    array = jax.random.normal(own_key, extent, jnp.float32) * scale
    if len(pieces) > 0:
        array = block_levels(own_key, extent, pieces, -0.22, 0.18) * array
    return jnp.clip(array, min=-reach, max=reach).astype(kind)


def setup_inputs(seed: int = 0) -> dict:
    arg_keys = jax.random.split(jax.random.key(seed), 8)
    return {
        "conc_start": jnp.clip(0.5 + 1.5 * jax.random.uniform(arg_keys[0], (NX, NY, LZ), jnp.float32) ** block_levels(arg_keys[0], (NX, NY, LZ), ((0, 8), (1, 4)), -0.2, 0.2), 0.5, 2.0),
        "diffusion": jnp.clip(jnp.exp(math.log(0.12) - 1.3862944 * jax.random.uniform(arg_keys[1], (NX, NY, LZ), jnp.float32) ** block_levels(arg_keys[1], (NX, NY, LZ), ((0, 8), (1, 4)), -0.2, 0.2)), 0.03, 0.12),
        "courant": jnp.clip(jnp.exp(math.log(0.25) - 1.609438 * jax.random.uniform(arg_keys[2], (NX, NY, LZ), jnp.float32) ** block_levels(arg_keys[2], (NX, NY, LZ), ((0, 8), (1, 4)), -0.2, 0.2)), 0.05, 0.25),
        "uptake": jnp.clip(jnp.exp(math.log(0.2) - 2.3025851 * jax.random.uniform(arg_keys[3], (NX, NY, LZ), jnp.float32) ** block_levels(arg_keys[3], (NX, NY, LZ), ((0, 8), (1, 4)), -0.2, 0.2)), 0.02, 0.2),
        "directions": centred(arg_keys[4], (NDIR, NX, NY, LZ), 1.0, 6.0, ((1, 8), (2, 4)), jnp.float32),
        "sensor_cell": with_ends(jax.random.randint(arg_keys[5], (N_GX, N_GY, S_DEV), 0, CX * CY * LZ), jax.random.fold_in(arg_keys[5], 1), 0, (CX * CY * LZ) - 1).astype(jnp.int32),
        "sensor_step": with_ends(jax.random.randint(arg_keys[6], (N_GX, N_GY, S_DEV), 1, STEPS + 1), jax.random.fold_in(arg_keys[6], 1), 1, STEPS).astype(jnp.int32),
    }


HALF_SATURATION = 0.5
PRIOR_WEIGHT = 0.2
PRIOR_SHIFT = 0.5


def pad_sides(field):
    widths = [(0, 0)] * (field.ndim - 3) + [(1, 1), (1, 1), (0, 0)]
    return jnp.pad(field, widths)


def spread(padded):
    inner = padded[..., 1:-1, 1:-1, :]
    column = jnp.pad(inner, [(0, 0)] * (inner.ndim - 1) + [(1, 1)])
    beside = padded[..., 2:, 1:-1, :] + padded[..., :-2, 1:-1, :]
    beside = beside + padded[..., 1:-1, 2:, :] + padded[..., 1:-1, :-2, :]
    beside = beside + column[..., 2:] + column[..., :-2]
    return inner, beside


def lifted(field):
    return jnp.pad(field, [(0, 0)] * (field.ndim - 1) + [(1, 0)])[..., :-1]


def dropped(field):
    return jnp.pad(field, [(0, 0)] * (field.ndim - 1) + [(0, 1)])[..., 1:]


def base_step(padded, diffusion, courant, uptake):
    inner, beside = spread(padded)
    carried = courant * inner
    return inner + diffusion * (beside - 6.0 * inner) + lifted(carried) - carried - uptake * inner / (HALF_SATURATION + inner)


def tangent_step(padded, diffusion, courant, linear, source):
    inner, beside = spread(padded)
    carried = courant * inner
    return inner + diffusion * (beside - 6.0 * inner) + lifted(carried) - carried - linear * inner - source


def adjoint_step(padded, adjoint, courant, linear):
    inner_q, beside_q = spread(padded)
    return adjoint + beside_q - 6.0 * inner_q + courant * (dropped(adjoint) - adjoint) - linear * adjoint


def reference(conc_start, diffusion, courant, uptake, directions, sensor_cell, sensor_step):
    states = [conc_start]
    current = conc_start
    for step in range(STEPS):
        current = base_step(pad_sides(current), diffusion, courant, uptake)
        states.append(current)
    ratios = [s / (HALF_SATURATION + s) for s in states[:STEPS]]
    linears = [uptake * HALF_SATURATION / ((HALF_SATURATION + s) * (HALF_SATURATION + s)) for s in states[:STEPS]]
    rows_x = sensor_cell // (CY * LZ)
    rows_y = (sensor_cell // LZ) % CY
    layer = sensor_cell % LZ
    base_x = jnp.arange(N_GX, dtype=jnp.int32)[:, None, None] * CX
    base_y = jnp.arange(N_GY, dtype=jnp.int32)[None, :, None] * CY
    cells = (((base_x + rows_x) * NY + base_y + rows_y) * LZ + layer).reshape(-1).astype(jnp.int32)
    when = sensor_step.reshape(-1)

    def single(direction):
        tangent = -(direction * ratios[0])
        observed = []
        for step in range(1, STEPS + 1):
            if step > 1:
                tangent = tangent_step(pad_sides(tangent), diffusion, courant, linears[step - 1], direction * ratios[step - 1])
            values = tangent.reshape(-1)[cells]
            observed.append(jnp.where(when == step, values, jnp.float32(0.0)))
        adjoint = jnp.zeros((NX * NY * LZ,), jnp.float32).at[cells].add(observed[STEPS - 1]).reshape(NX, NY, LZ)
        gradient = jnp.zeros((NX, NY, LZ), jnp.float32)
        for step in range(STEPS - 1, -1, -1):
            gradient = gradient - ratios[step] * adjoint
            if step > 0:
                adjoint = adjoint_step(pad_sides(diffusion * adjoint), adjoint, courant, linears[step])
                adjoint = adjoint.reshape(-1).at[cells].add(observed[step - 1]).reshape(NX, NY, LZ)
        inner, beside = spread(pad_sides(direction))
        return gradient + PRIOR_WEIGHT * ((6.0 + PRIOR_SHIFT) * inner - beside)

    return lax.map(single, directions)
```

```python
import functools

import jax
import jax.numpy as jnp
from jax import lax
from jax.experimental import pallas as pl
from jax.experimental.pallas import tpu as pltpu
from jax.sharding import PartitionSpec as P

STEPS = 4
REACH = STEPS - 1
HALF_SATURATION = 0.5
PRIOR_WEIGHT = 0.2
PRIOR_SHIFT = 0.5
HALVES = 2
TILE = 8

MESH = pl.DeviceIdType.MESH

NEIGHBOURS = ((-1, 0), (1, 0), (0, -1), (0, 1), (-1, -1), (1, 1), (-1, 1), (1, -1))
OWN = (0, 0)
BLOCKS = (*NEIGHBOURS, OWN)
PAIRS = 5

A1, A2, A3, DZ, BU, DL, DC, R0, R1, R2, R3, N1, N2, N3, N4 = range(15)
C0, DD, UU, WW, C1, C2, C3 = range(7)


def place_of(block):
    k = BLOCKS.index(block)
    return (k // 2, k % 2)


def shared(d):
    return [b for b in BLOCKS if abs(b[0] - d[0]) <= 1 and abs(b[1] - d[1]) <= 1]


def kernel(
    sx, sy, depth,
    conc, diffusion, courant, uptake, dirs, cells, when, out,
    vp, t1, t2, t3, t4, a4, a3, a2, q4, q3, q2, pl3, pl2,
    ext, coefs, marks, ones, ii, zr, zi, acc, part, ysplit,
    s0, r0, s3, r3, s1, r1,
    s0_send, s0_recv, s3_send, s3_recv, v_send, v_recv, s1_send, s1_recv,
):
    layers = conc.shape[-1]
    half_lanes = layers // 2
    cols = sx * sy
    ex_n, ey_n = ext.shape[1], ext.shape[2]
    lo_x, hi_x, lo_y, hi_y = REACH, REACH + sx, REACH, REACH + sy
    ix, iy = lax.axis_index("gx"), lax.axis_index("gy")
    nx, ny = lax.axis_size("gx"), lax.axis_size("gy")
    have, partner = [], []
    for dx, dy in NEIGHBOURS:
        here = []
        if dx:
            here.append(ix > 0 if dx < 0 else ix < nx - 1)
        if dy:
            here.append(iy > 0 if dy < 0 else iy < ny - 1)
        have.append(functools.reduce(jnp.logical_and, here))
        px = jnp.maximum(ix - 1, 0) if dx < 0 else jnp.minimum(ix + 1, nx - 1) if dx > 0 else ix
        py = jnp.maximum(iy - 1, 0) if dy < 0 else jnp.minimum(iy + 1, ny - 1) if dy > 0 else iy
        partner.append((px, py))
    sides = range(4)
    every = range(8)

    def on(action, ks):
        for k in ks:
            @pl.when(have[k])
            def _(k=k):
                action(k)

    barrier = pltpu.get_barrier_semaphore()
    on(lambda k: pl.semaphore_signal(barrier, inc=1, device_id=partner[k], device_id_type=MESH), every)

    def remote(src, dst, send, recv, k):
        return pltpu.make_async_remote_copy(
            src_ref=src, dst_ref=dst, send_sem=send, recv_sem=recv, device_id=partner[k], device_id_type=MESH
        )

    def size0(k):
        return 1 + 4 * REACH if k < 4 else 3

    def copy0(k):
        n = pl.ds(0, size0(k))
        return remote(s0.at[k, n], r0.at[k ^ 1, n], s0_send.at[k], s0_recv.at[k ^ 1], k)

    def landed0(k):
        n = pl.ds(0, size0(k))
        return remote(r0.at[k, n], r0.at[k, n], s0_send.at[k], s0_recv.at[k], k)

    def size3(k):
        return 2 if k < 4 else 1

    def copy3(k):
        n = pl.ds(0, size3(k))
        return remote(s3.at[k, n], r3.at[k ^ 1, n], s3_send.at[k], s3_recv.at[k ^ 1], k)

    def landed3(k):
        n = pl.ds(0, size3(k))
        return remote(r3.at[k, n], r3.at[k, n], s3_send.at[k], s3_recv.at[k], k)

    def v_at(h, k, halo):
        if k == 0:
            return vp.at[h, 0 if halo else 1, pl.ds(1, sy)]
        if k == 1:
            return vp.at[h, sx + 1 if halo else sx, pl.ds(1, sy)]
        if k == 2:
            return vp.at[h, pl.ds(1, sx), 0 if halo else 1]
        return vp.at[h, pl.ds(1, sx), sy + 1 if halo else sy]

    def copy_v(h, k):
        return remote(v_at(h, k, False), v_at(h, k ^ 1, True), v_send.at[h, k], v_recv.at[h, k ^ 1], k)

    def landed_v(h, k):
        return remote(v_at(h, k, True), v_at(h, k, True), v_send.at[h, k], v_recv.at[h, k], k)

    def size1(k):
        return (len(shared(NEIGHBOURS[k])) + 1) // 2

    def copy1(h, k):
        n = pl.ds(0, size1(k))
        return remote(s1.at[h, k, n], r1.at[h, k ^ 1, n], s1_send.at[h, k], s1_recv.at[h, k ^ 1], k)

    def landed1(h, k):
        n = pl.ds(0, size1(k))
        return remote(r1.at[h, k, n], r1.at[h, k, n], s1_send.at[h, k], s1_recv.at[h, k], k)

    fields = (conc, diffusion, courant, uptake)
    sensors = cells.shape[1]
    ii[...] = jnp.full(ii.shape, -1, jnp.int32)
    ii[0:1, 0:sensors] = cells[...] // layers + cols * when[...]
    ii[1:2, 0:sensors] = cells[...] % layers
    lane8 = lax.broadcasted_iota(jnp.int32, ii.shape, 1)
    packed = ii[...]
    about = jnp.where(lane8 < half_lanes, packed, pltpu.roll(packed, half_lanes, 1)).astype(jnp.float32)
    for k in every:
        s0[k, 0] = about
    for f, field in enumerate(fields):
        block = field[...]
        for i in range(REACH):
            s0[0, 1 + f * REACH + i] = block[i]
            s0[1, 1 + f * REACH + i] = block[sx - REACH + i]
            for k, y in ((2, i), (3, sy - REACH + i)):
                s0[k, 1 + f * REACH + i] = jnp.concatenate([block[x, y:y + 1] for x in range(sx)], axis=0)
        for k in range(4, 8):
            dx, dy = NEIGHBOURS[k]
            for i in range(2):
                for j in range(2):
                    x, y = (i if dx < 0 else sx - 2 + i), (j if dy < 0 else sy - 2 + j)
                    r = f * 4 + i * 2 + j
                    s0[k, 1 + r // TILE, r % TILE:r % TILE + 1] = block[x, y:y + 1]

    pl.semaphore_wait(barrier, sum(jnp.where(here, 1, 0) for here in have))
    on(lambda k: copy0(k).start(), every)

    for h in range(HALVES):
        @pl.loop(0, sx)
        def _(x, h=h):
            for y in range(sy):
                vp[h, x + 1, y + 1] = dirs[pl.ds(h * depth * cols + x * sy + y, depth, stride=cols), :]
        if h == 0:
            on(lambda k: copy_v(0, k).start(), sides)

    for k in every:
        @pl.when(jnp.logical_not(have[k]))
        def _(k=k):
            r0[k] = jnp.zeros(r0.shape[1:], jnp.float32)
            r3[k] = jnp.zeros(r3.shape[1:], jnp.float32)
            for h in range(HALVES):
                r1[h, k] = jnp.zeros(r1.shape[2:], jnp.float32)
                if k < 4:
                    ref = v_at(h, k, True)
                    ref[...] = jnp.zeros(ref.shape, jnp.float32)

    blank = jnp.zeros((depth, layers), jnp.float32)
    for h in range(HALVES):
        for X in (lo_x - 1, hi_x):
            for Y in range(lo_y, hi_y):
                t1[h, X, Y] = blank
            for Y in (lo_y - 1, hi_y):
                t2[h, X, Y] = blank
            for Y in (lo_y - 2, hi_y + 1):
                t3[h, X, Y] = blank
    for X in range(lo_x, hi_x):
        for Y in range(lo_y, hi_y):
            pl3[X, Y] = blank
            pl2[X, Y] = blank
    for f in range(4):
        ext[f] = jnp.zeros(ext.shape[1:], jnp.float32)
    for k in (A1, A2, A3):
        coefs[k] = jnp.zeros(coefs.shape[1:], jnp.float32)
    for f, field in enumerate(fields):
        for x in range(sx):
            ext[f, lo_x + x, pl.ds(lo_y, sy), :] = field[x]

    for X in range(lo_x, hi_x):
        c = ext[C0, X]
        coefs[R0, X] = c / (HALF_SATURATION + c)

    def coef(k, X, Y):
        return coefs[k, X, pl.ds(Y, 1), :]

    def dcoef(X, Y):
        return ext[DD, X, pl.ds(Y, 1), :]

    for h in range(HALVES):
        @pl.loop(lo_x, hi_x)
        def _(X, h=h):
            for Y in range(lo_y, hi_y):
                t1[h, X, Y] = -(vp[h, X - lo_x + 1, Y - lo_y + 1] * coef(R0, X, Y))

    on(lambda k: landed0(k).wait_recv(), every)

    for f in range(4):
        for i in range(REACH):
            ext[f, i, pl.ds(lo_y, sy), :] = r0[0, 1 + f * REACH + i]
            ext[f, hi_x + i, pl.ds(lo_y, sy), :] = r0[1, 1 + f * REACH + i]
            for k, Y in ((2, i), (3, hi_y + i)):
                strip = r0[k, 1 + f * REACH + i]
                for x in range(sx):
                    ext[f, lo_x + x, Y:Y + 1, :] = strip[x:x + 1]
        for k in range(4, 8):
            dx, dy = NEIGHBOURS[k]
            for i in range(2):
                for j in range(2):
                    X, Y = (lo_x - 2 + i if dx < 0 else hi_x + i), (lo_y - 2 + j if dy < 0 else hi_y + j)
                    r = f * 4 + i * 2 + j
                    ext[f, X, Y:Y + 1, :] = r0[k, 1 + r // TILE, r % TILE:r % TILE + 1]

    layer = lax.broadcasted_iota(jnp.int32, (ey_n, layers), 1)
    first, last = layer == 0, layer == layers - 1

    def lift(f):
        return jnp.where(first, 0.0, pltpu.roll(f, 1, 1))

    def drop(f):
        return jnp.where(last, 0.0, pltpu.roll(f, layers - 1, 1))

    def next_conc(now, later, margin, tail=None):
        @pl.loop(margin, ex_n - margin)
        def _(X):
            c, d, u, w = ext[now, X], ext[DD, X], ext[UU, X], ext[WW, X]
            beside = (
                ext[now, X - 1] + ext[now, X + 1] + pltpu.roll(c, 1, 0) + pltpu.roll(c, ey_n - 1, 0)
                + lift(c) + drop(c)
            )
            carried = u * c
            new = c + d * (beside - 6.0 * c) + lift(carried) - carried - w * c / (HALF_SATURATION + c)
            ext[later, X] = new
            held = HALF_SATURATION + new
            coefs[R1 + later - C1, X] = new / held
            coefs[A1 + later - C1, X] = 1.0 - 6.0 * d - u - w * HALF_SATURATION / (held * held)

    next_conc(C0, C1, 1)
    next_conc(C1, C2, 2)
    next_conc(C2, C3, 3)

    for i in range(2):
        s3[0, i] = coefs[A3, lo_x + i, pl.ds(lo_y, sy), :]
        s3[1, i] = coefs[A3, hi_x - 2 + i, pl.ds(lo_y, sy), :]
        for k, Y in ((2, lo_y + i), (3, hi_y - 2 + i)):
            for x in range(sx):
                s3[k, i, x:x + 1] = coefs[A3, lo_x + x, Y:Y + 1, :]
    for k in range(4, 8):
        dx, dy = NEIGHBOURS[k]
        X, Y = (lo_x if dx < 0 else hi_x - 1), (lo_y if dy < 0 else hi_y - 1)
        s3[k, 0] = jnp.broadcast_to(coefs[A3, X, Y:Y + 1, :], (TILE, layers))
    on(lambda k: copy3(k).start(), every)
    on(lambda k: copy_v(1, k).start(), sides)

    @pl.loop(1, ex_n - 1)
    def _(X):
        d, u = ext[DD, X], ext[UU, X]
        coefs[DZ, X] = jnp.where(last, 0.0, d)
        coefs[BU, X] = jnp.where(first, 0.0, d) + lift(u)
        coefs[DL, X] = lift(d)
        coefs[DC, X] = drop(d) + jnp.where(last, 0.0, u)

    lane1 = lax.broadcasted_iota(jnp.int32, (1, layers), 1)
    keys, depths = {}, {}
    for k, b in enumerate(BLOCKS):
        tile = r0[k, 0] if k < 8 else s0[0, 0]
        low = place_of(b)[1] == 0
        keys[b] = jnp.where((lane1 < half_lanes) == low, tile[0:1], -1.0)
        depths[b] = tile[1:2]
    level = lax.broadcasted_iota(jnp.int32, (layers, layers), 0).astype(jnp.float32)
    for p in range(PAIRS):
        pair = BLOCKS[2 * p:2 * p + 2]
        where = jnp.where(lane1 < half_lanes, depths[pair[0]], depths[pair[-1]])
        hot = jnp.where(level == where, 1.0, 0.0).astype(jnp.bfloat16)
        zr[p, 0:layers] = hot
        zr[p, layers:2 * layers] = hot
        zi[p, :, 0:layers] = hot
        zi[p, :, layers:2 * layers] = hot
    yrow = lax.broadcasted_iota(jnp.int32, (ey_n, layers), 0)
    ymod = (yrow + (sy - REACH % sy)) % sy
    key_at = {
        dx: jnp.where(yrow < lo_y, keys[(dx, -1)], jnp.where(yrow < hi_y, keys[(dx, 0)], keys[(dx, 1)]))
        for dx in (-1, 0, 1)
    }
    for X in range(ex_n):
        dx = -1 if X < lo_x else 1 if X >= hi_x else 0
        name = (((X - REACH) % sx) * sy + ymod).astype(jnp.float32)
        for t in range(1, STEPS + 1):
            mark = jnp.where(key_at[dx] == name + float(cols * t), 1.0, 0.0)
            if t > 1:
                marks[t - 2, X] = mark
            elif dx == 0:
                ones[X - lo_x] = mark
    for t in range(1, STEPS + 1):
        mark = ones[...] if t == 1 else marks[t - 2, pl.ds(lo_x, sx)]
        count = lax.dot_general(
            mark.reshape(sx * ey_n, layers).astype(jnp.bfloat16), zi[PAIRS - 1, :, 0:layers],
            (((1,), (1,)), ((), ())), preferred_element_type=jnp.float32,
        )
        coefs[N1 + t - 1, pl.ds(lo_x, sx)] = count.reshape(sx, ey_n, layers)

    def up(f):
        return pltpu.roll(f, 1, 1)

    def down(f):
        return pltpu.roll(f, layers - 1, 1)

    def add(terms):
        return functools.reduce(lambda p, q: p + q, terms)

    def rows(reach, body):
        @pl.loop(lo_x, hi_x)
        def _(X):
            body(X, 0, 0)
        for j in range(1, reach + 1):
            @pl.loop(0, 2)
            def _(side, j=j):
                body(lo_x - j + side * (sx + 2 * j - 1), j, 1 - 2 * side)

    def out_y(Y):
        return max(0, lo_y - Y, Y - hi_y + 1)

    def tangent_row(h, reach, prev, new, ka, kr, X, ex, inward):
        held = reach - 1
        mid = {}
        if ex <= held:
            mid = {Y: prev[h, X, Y] for Y in range(lo_y - held + ex, hi_y + held - ex)}
        for Y in range(lo_y - reach + ex, hi_y + reach - ex):
            ey = out_y(Y)
            terms = [mid[near] for near in (Y - 1, Y + 1) if near in mid]
            if ex == 0:
                if ey <= held:
                    terms += [prev[h, X - 1, Y], prev[h, X + 1, Y]]
            else:
                terms.append(prev[h, X + inward, Y])
                if ex + 1 + ey <= held:
                    terms.append(prev[h, X - inward, Y])
            value = dcoef(X, Y) * add(terms)
            if ex + ey < reach:
                p = mid[Y]
                value = (
                    value + coef(ka, X, Y) * p + coef(DZ, X, Y) * down(p) + coef(BU, X, Y) * up(p)
                )
                if ex == 0 and ey == 0:
                    value = value - coef(kr, X, Y) * vp[h, X - lo_x + 1, Y - lo_y + 1]
            new[h, X, Y] = value

    def block_of(X, Y):
        return (
            -1 if X < lo_x else 1 if X >= hi_x else 0,
            -1 if Y < lo_y else 1 if Y >= hi_y else 0,
        )

    def touched(p, reach):
        found = []
        for X in range(ex_n):
            for Y in range(lo_y + sy + REACH):
                b = block_of(X, Y)
                if place_of(b)[0] != p:
                    continue
                if b == OWN:
                    near = min(X - lo_x, hi_x - 1 - X, Y - lo_y, hi_y - 1 - Y) < reach
                else:
                    near = max(0, lo_x - X, X - hi_x + 1) + out_y(Y) <= reach
                if near:
                    found.append((X, Y))
        return found

    chunk = 16

    def read(h, p, wanted):
        total = None
        for start in range(0, len(wanted), chunk):
            some = wanted[start:start + chunk]
            high, low = [], []
            for field, t, X, Y in some:
                value = field[h, X, Y]
                top = value.astype(jnp.bfloat16)
                high.append(top)
                low.append((value - top.astype(jnp.float32)).astype(jnp.bfloat16))
            left = jnp.concatenate([jnp.concatenate(high, axis=0), jnp.concatenate(low, axis=0)], axis=1)
            got = lax.dot_general(left, zr[p], (((1,), (0,)), ((), ())), preferred_element_type=jnp.float32)
            for i, (field, t, X, Y) in enumerate(some):
                term = got[i * depth:(i + 1) * depth] * marks[t - 2, X, pl.ds(Y, 1), :]
                total = term if total is None else total + term
        return total

    @pl.loop(0, HALVES)
    def _(h):
        rows(1, functools.partial(tangent_row, h, 1, t1, t2, A1, R1))
        rows(2, functools.partial(tangent_row, h, 2, t2, t3, A2, R2))
        for p in range(PAIRS):
            acc[h, p] = read(
                h, p, [(t2, 2, *at) for at in touched(p, 1)] + [(t3, 3, *at) for at in touched(p, 2)]
            )

    on(lambda k: landed3(k).wait_recv(), every)
    for i in range(2):
        coefs[A3, lo_x - 2 + i, pl.ds(lo_y, sy), :] = r3[0, i]
        coefs[A3, hi_x + i, pl.ds(lo_y, sy), :] = r3[1, i]
        for k, Y in ((2, lo_y - 2 + i), (3, hi_y + i)):
            for x in range(sx):
                coefs[A3, lo_x + x, Y:Y + 1, :] = r3[k, i, x:x + 1]
    for k in range(4, 8):
        dx, dy = NEIGHBOURS[k]
        X, Y = (lo_x - 1 if dx < 0 else hi_x), (lo_y - 1 if dy < 0 else hi_y)
        coefs[A3, X, Y:Y + 1, :] = r3[k, 0, 0:1]

    lane = lax.broadcasted_iota(jnp.int32, (depth, layers), 1)
    lower = lane < half_lanes

    def moved(value, source, target):
        return value if source == target else pltpu.roll(value, half_lanes, 1)

    @pl.loop(0, HALVES)
    def _(h):
        rows(3, functools.partial(tangent_row, h, 3, t3, t4, A3, R3))
        mine = []
        for p in range(PAIRS):
            mine.append(acc[h, p] + read(h, p, [(t4, 4, *at) for at in touched(p, 3)]))
            part[h, p] = mine[p]
        for k, d in enumerate(NEIGHBOURS):
            need = shared(d)
            for j in range(0, len(need), 2):
                (pa, ha), (pb, hb) = place_of(need[j]), place_of(need[j + 1])
                s1[h, k, j // 2] = jnp.where(lower, moved(mine[pa], ha, 0), moved(mine[pb], hb, 1))
        on(lambda k: copy1(h, k).start(), every)

    for h in range(HALVES):
        on(lambda k: landed_v(h, k).wait_recv(), sides)
    not_first = jnp.where(lane1 == 0, 0.0, 1.0)
    not_last = jnp.where(lane1 == layers - 1, 0.0, 1.0)

    @pl.loop(0, HALVES)
    def _(h):
        @pl.loop(0, sx)
        def _(x):
            X = x + lo_x
            mid = [vp[h, x + 1, y] for y in range(sy + 2)]
            for y in range(sy):
                Y = y + lo_y
                v = mid[y + 1]
                beside = (
                    (vp[h, x, y + 1] + vp[h, x + 2, y + 1]) + (mid[y] + mid[y + 2])
                    + not_first * up(v) + not_last * down(v)
                )
                first_sensors = coef(R0, X, Y) * (coef(N1, X, Y) * t1[h, X, Y])
                out[x * sy + y, pl.ds(h * depth, depth)] = (
                    PRIOR_WEIGHT * ((6.0 + PRIOR_SHIFT) * v - beside) - first_sensors
                )

    def inject(p, t, reach, use):
        wanted = touched(p, reach)
        for start in range(0, len(wanted), chunk):
            some = wanted[start:start + chunk]
            high, low = [], []
            for X, Y in some:
                mark = jnp.broadcast_to(marks[t - 2, X, pl.ds(Y, 1), :], (depth, layers)).astype(jnp.bfloat16)
                high.append(ysplit[p, 0] * mark)
                low.append(ysplit[p, 1] * mark)
            left = jnp.concatenate([jnp.concatenate(high, axis=0), jnp.concatenate(low, axis=0)], axis=1)
            got = lax.dot_general(left, zi[p], (((1,), (1,)), ((), ())), preferred_element_type=jnp.float32)
            for i, (X, Y) in enumerate(some):
                use(X, Y, got[i * depth:(i + 1) * depth])

    def adjoint(hold, q, ka, X, Y, centre):
        a = hold[X, Y] if centre is None else centre
        return (
            coef(ka, X, Y) * a
            + ((q[X - 1, Y] + q[X + 1, Y]) + (q[X, Y - 1] + q[X, Y + 1]))
            + coef(DL, X, Y) * up(a)
            + coef(DC, X, Y) * down(a)
        )

    def adjoint_row(h, reach, hold, q, new_hold, new_q, placed, tangent, ka, kn, X, ex, inward):
        for Y in range(lo_y - reach + ex, hi_y + reach - ex):
            a = adjoint(hold, q, ka, X, Y, None) + placed[X, Y]
            if ex == 0 and out_y(Y) == 0:
                a = a + coef(kn, X, Y) * tangent[h, X, Y]
            new_hold[X, Y] = a
            new_q[X, Y] = dcoef(X, Y) * a

    inner = [
        (X, Y) for X in range(lo_x, hi_x) for Y in range(lo_y, hi_y) if (X, Y) not in touched(PAIRS - 1, 3)
    ]

    @pl.loop(0, HALVES)
    def _(h):
        on(lambda k: landed1(h, k).wait_recv(), every)
        total = [part[h, p] for p in range(PAIRS - 1)] + [blank]
        for k, d in enumerate(NEIGHBOURS):
            need = shared(NEIGHBOURS[k ^ 1])
            for j, b in enumerate(need):
                p, target = place_of((b[0] + d[0], b[1] + d[1]))
                value = moved(r1[h, k, j // 2], j % 2, target)
                total[p] = total[p] + jnp.where(lower == (target == 0), value, 0.0)
        for p in range(PAIRS):
            top = total[p].astype(jnp.bfloat16)
            ysplit[p, 0] = top
            ysplit[p, 1] = (total[p] - top.astype(jnp.float32)).astype(jnp.bfloat16)

        def last_step(X, Y, value):
            a4[X, Y] = value
            q4[X, Y] = dcoef(X, Y) * value

        def last_own(X, Y, value):
            last_step(X, Y, value + coef(N4, X, Y) * t4[h, X, Y])

        def to_three(X, Y, value):
            pl3[X, Y] = value

        def to_two(X, Y, value):
            pl2[X, Y] = value

        for p in range(PAIRS):
            inject(p, 4, 3, last_own if p == PAIRS - 1 else last_step)
            inject(p, 3, 2, to_three)
            inject(p, 2, 1, to_two)
        for X, Y in inner:
            last_step(X, Y, coef(N4, X, Y) * t4[h, X, Y])
        rows(2, functools.partial(adjoint_row, h, 2, a4, q4, a3, q3, pl3, t3, A3, N3))
        rows(1, functools.partial(adjoint_row, h, 1, a3, q3, a2, q2, pl2, t2, A2, N2))

        @pl.loop(0, sx)
        def _(x):
            X = x + lo_x
            for y in range(sy):
                Y = y + lo_y
                middle = a2[X, Y]
                gradient = (
                    coef(R3, X, Y) * a4[X, Y] + coef(R2, X, Y) * a3[X, Y] + coef(R1, X, Y) * middle
                    + coef(R0, X, Y) * adjoint(a2, q2, A1, X, Y, middle)
                )
                at = (x * sy + y, pl.ds(h * depth, depth))
                out[at] = out[at] - gradient

    on(lambda k: copy0(k).wait_send(), every)
    on(lambda k: copy3(k).wait_send(), every)
    for h in range(HALVES):
        on(lambda k: copy_v(h, k).wait_send(), sides)
        on(lambda k: copy1(h, k).wait_send(), every)


def on_device(conc_start, diffusion, courant, uptake, directions, sensor_cell, sensor_step):
    count_dir, sx, sy, layers = directions.shape
    depth = count_dir // HALVES
    sensors = sensor_cell.shape[-1]
    assert sensors <= layers // 2 and min(sx, sy) >= 2 * REACH and depth % 16 == 0
    ex_n, ey_n = sx + 2 * REACH, pl.cdiv(sy + 2 * REACH, TILE) * TILE
    vmem = pltpu.VMEM
    wide = sy + 2 * REACH
    both = vmem((HALVES, ex_n, wide, depth, layers), jnp.float32)
    one = vmem((ex_n, wide, depth, layers), jnp.float32)

    def table(n):
        return vmem((n, ex_n, ey_n, layers), jnp.float32)

    tiles = 1 + 4 * REACH
    sems = pltpu.SemaphoreType.DMA
    result = pl.pallas_call(
        functools.partial(kernel, sx, sy, depth),
        out_shape=jax.ShapeDtypeStruct((sx * sy, count_dir, layers), jnp.float32),
        in_specs=[pl.BlockSpec(memory_space=vmem)] * 7,
        out_specs=pl.BlockSpec(memory_space=vmem),
        scratch_shapes=[
            vmem((HALVES, sx + 2, sy + 2, depth, layers), jnp.float32),
            *[both] * 4,
            *[one] * 8,
            table(7),
            table(15),
            table(STEPS - 1),
            vmem((sx, ey_n, layers), jnp.float32),
            vmem((TILE, layers), jnp.int32),
            vmem((PAIRS, 2 * layers, layers), jnp.bfloat16),
            vmem((PAIRS, layers, 2 * layers), jnp.bfloat16),
            vmem((HALVES, PAIRS, depth, layers), jnp.float32),
            vmem((HALVES, PAIRS, depth, layers), jnp.float32),
            vmem((PAIRS, 2, depth, layers), jnp.bfloat16),
            vmem((8, tiles, TILE, layers), jnp.float32),
            vmem((8, tiles, TILE, layers), jnp.float32),
            vmem((8, 2, TILE, layers), jnp.float32),
            vmem((8, 2, TILE, layers), jnp.float32),
            vmem((HALVES, 8, 3, depth, layers), jnp.float32),
            vmem((HALVES, 8, 3, depth, layers), jnp.float32),
            sems((8,)), sems((8,)),
            sems((8,)), sems((8,)),
            sems((HALVES, 4)), sems((HALVES, 4)),
            sems((HALVES, 8)), sems((HALVES, 8)),
        ],
        compiler_params=pltpu.CompilerParams(
            collective_id=0, has_side_effects=True, vmem_limit_bytes=56 * 2**20
        ),
    )(
        conc_start, diffusion, courant, uptake,
        directions.reshape(count_dir * sx * sy, layers),
        sensor_cell.reshape(1, sensors), sensor_step.reshape(1, sensors),
    )
    return jnp.swapaxes(result, 0, 1).reshape(count_dir, sx, sy, layers)


def solution(mesh):
    in_specs = (
        P("gx", "gy", None),
        P("gx", "gy", None),
        P("gx", "gy", None),
        P("gx", "gy", None),
        P(None, "gx", "gy", None),
        P("gx", "gy", None),
        P("gx", "gy", None),
    )
    out_specs = P(None, "gx", "gy", None)
    return jax.shard_map(
        on_device, mesh=mesh, in_specs=in_specs, out_specs=out_specs, check_vma=False
    )
```

```python
import functools

import jax
import jax.numpy as jnp
from jax import lax
from jax.experimental import pallas as pl
from jax.experimental.pallas import tpu as pltpu
from jax.sharding import PartitionSpec as P

STEPS = 4
REACH = STEPS - 1
HALF_SATURATION = 0.5
PRIOR_WEIGHT = 0.2
PRIOR_SHIFT = 0.5
HALVES = 2
TILE = 8

MESH = pl.DeviceIdType.MESH

NEIGHBOURS = ((-1, 0), (1, 0), (0, -1), (0, 1), (-1, -1), (1, 1), (-1, 1), (1, -1))
OWN = (0, 0)
BLOCKS = (*NEIGHBOURS, OWN)
PAIRS = 5

A1, A2, A3, DZ, BU, DL, DC, R0, R1, R2, R3, N1, N2, N3, N4 = range(15)
C0, DD, UU, WW, C1, C2, C3 = range(7)


def place_of(block):
    k = BLOCKS.index(block)
    return (k // 2, k % 2)


def shared(d):
    return [b for b in BLOCKS if abs(b[0] - d[0]) <= 1 and abs(b[1] - d[1]) <= 1]


def kernel(
    sx, sy, depth,
    conc, diffusion, courant, uptake, dirs, cells, when, out,
    vp, t1, t2, t3, t4, a4, a3, a2, q4, q3, q2, pl3, pl2,
    ext, coefs, marks, ones, ii, zr, zi, acc, part, ysplit,
    s0, r0, s3, r3, s1, r1,
    s0_send, s0_recv, s3_send, s3_recv, v_send, v_recv, s1_send, s1_recv,
):
    layers = conc.shape[-1]
    half_lanes = layers // 2
    cols = sx * sy
    ex_n, ey_n = ext.shape[1], ext.shape[2]
    lo_x, hi_x, lo_y, hi_y = REACH, REACH + sx, REACH, REACH + sy
    ix, iy = lax.axis_index("gx"), lax.axis_index("gy")
    nx, ny = lax.axis_size("gx"), lax.axis_size("gy")
    have, partner = [], []
    for dx, dy in NEIGHBOURS:
        here = []
        if dx:
            here.append(ix > 0 if dx < 0 else ix < nx - 1)
        if dy:
            here.append(iy > 0 if dy < 0 else iy < ny - 1)
        have.append(functools.reduce(jnp.logical_and, here))
        px = jnp.maximum(ix - 1, 0) if dx < 0 else jnp.minimum(ix + 1, nx - 1) if dx > 0 else ix
        py = jnp.maximum(iy - 1, 0) if dy < 0 else jnp.minimum(iy + 1, ny - 1) if dy > 0 else iy
        partner.append((px, py))
    sides = range(4)
    every = range(8)

    def on(action, ks):
        for k in ks:
            @pl.when(have[k])
            def _(k=k):
                action(k)

    barrier = pltpu.get_barrier_semaphore()
    on(lambda k: pl.semaphore_signal(barrier, inc=1, device_id=partner[k], device_id_type=MESH), every)

    def remote(src, dst, send, recv, k):
        return pltpu.make_async_remote_copy(
            src_ref=src, dst_ref=dst, send_sem=send, recv_sem=recv, device_id=partner[k], device_id_type=MESH
        )

    def size0(k):
        return 1 + 4 * REACH if k < 4 else 3

    def copy0(k):
        n = pl.ds(0, size0(k))
        return remote(s0.at[k, n], r0.at[k ^ 1, n], s0_send.at[k], s0_recv.at[k ^ 1], k)

    def landed0(k):
        n = pl.ds(0, size0(k))
        return remote(r0.at[k, n], r0.at[k, n], s0_send.at[k], s0_recv.at[k], k)

    def size3(k):
        return 2 if k < 4 else 1

    def copy3(k):
        n = pl.ds(0, size3(k))
        return remote(s3.at[k, n], r3.at[k ^ 1, n], s3_send.at[k], s3_recv.at[k ^ 1], k)

    def landed3(k):
        n = pl.ds(0, size3(k))
        return remote(r3.at[k, n], r3.at[k, n], s3_send.at[k], s3_recv.at[k], k)

    def v_at(h, k, halo):
        if k == 0:
            return vp.at[h, 0 if halo else 1, pl.ds(1, sy)]
        if k == 1:
            return vp.at[h, sx + 1 if halo else sx, pl.ds(1, sy)]
        if k == 2:
            return vp.at[h, pl.ds(1, sx), 0 if halo else 1]
        return vp.at[h, pl.ds(1, sx), sy + 1 if halo else sy]

    def copy_v(h, k):
        return remote(v_at(h, k, False), v_at(h, k ^ 1, True), v_send.at[h, k], v_recv.at[h, k ^ 1], k)

    def landed_v(h, k):
        return remote(v_at(h, k, True), v_at(h, k, True), v_send.at[h, k], v_recv.at[h, k], k)

    def size1(k):
        return (len(shared(NEIGHBOURS[k])) + 1) // 2

    def copy1(h, k):
        n = pl.ds(0, size1(k))
        return remote(s1.at[h, k, n], r1.at[h, k ^ 1, n], s1_send.at[h, k], s1_recv.at[h, k ^ 1], k)

    def landed1(h, k):
        n = pl.ds(0, size1(k))
        return remote(r1.at[h, k, n], r1.at[h, k, n], s1_send.at[h, k], s1_recv.at[h, k], k)

    fields = (conc, diffusion, courant, uptake)
    sensors = cells.shape[1]
    ii[...] = jnp.full(ii.shape, -1, jnp.int32)
    ii[0:1, 0:sensors] = cells[...] // layers + cols * when[...]
    ii[1:2, 0:sensors] = cells[...] % layers
    lane8 = lax.broadcasted_iota(jnp.int32, ii.shape, 1)
    packed = ii[...]
    about = jnp.where(lane8 < half_lanes, packed, pltpu.roll(packed, half_lanes, 1)).astype(jnp.float32)
    for k in every:
        s0[k, 0] = about
    for f, field in enumerate(fields):
        block = field[...]
        for i in range(REACH):
            s0[0, 1 + f * REACH + i] = block[i]
            s0[1, 1 + f * REACH + i] = block[sx - REACH + i]
            for k, y in ((2, i), (3, sy - REACH + i)):
                s0[k, 1 + f * REACH + i] = jnp.concatenate([block[x, y:y + 1] for x in range(sx)], axis=0)
        for k in range(4, 8):
            dx, dy = NEIGHBOURS[k]
            for i in range(2):
                for j in range(2):
                    x, y = (i if dx < 0 else sx - 2 + i), (j if dy < 0 else sy - 2 + j)
                    r = f * 4 + i * 2 + j
                    s0[k, 1 + r // TILE, r % TILE:r % TILE + 1] = block[x, y:y + 1]

    pl.semaphore_wait(barrier, sum(jnp.where(here, 1, 0) for here in have))
    on(lambda k: copy0(k).start(), every)

    for h in range(HALVES):
        @pl.loop(0, sx)
        def _(x, h=h):
            for y in range(sy):
                vp[h, x + 1, y + 1] = dirs[pl.ds(h * depth * cols + x * sy + y, depth, stride=cols), :]
        if h == 0:
            on(lambda k: copy_v(0, k).start(), sides)

    for k in every:
        @pl.when(jnp.logical_not(have[k]))
        def _(k=k):
            r0[k] = jnp.zeros(r0.shape[1:], jnp.float32)
            r3[k] = jnp.zeros(r3.shape[1:], jnp.float32)
            for h in range(HALVES):
                r1[h, k] = jnp.zeros(r1.shape[2:], jnp.float32)
                if k < 4:
                    ref = v_at(h, k, True)
                    ref[...] = jnp.zeros(ref.shape, jnp.float32)

    blank = jnp.zeros((depth, layers), jnp.float32)
    for h in range(HALVES):
        for X in (lo_x - 1, hi_x):
            for Y in range(lo_y, hi_y):
                t1[h, X, Y] = blank
            for Y in (lo_y - 1, hi_y):
                t2[h, X, Y] = blank
            for Y in (lo_y - 2, hi_y + 1):
                t3[h, X, Y] = blank
    for X in range(lo_x, hi_x):
        for Y in range(lo_y, hi_y):
            pl3[X, Y] = blank
            pl2[X, Y] = blank
    for f in range(4):
        ext[f] = jnp.zeros(ext.shape[1:], jnp.float32)
    for k in (A1, A2, A3):
        coefs[k] = jnp.zeros(coefs.shape[1:], jnp.float32)
    for f, field in enumerate(fields):
        for x in range(sx):
            ext[f, lo_x + x, pl.ds(lo_y, sy), :] = field[x]

    for X in range(lo_x, hi_x):
        c = ext[C0, X]
        coefs[R0, X] = c / (HALF_SATURATION + c)

    def coef(k, X, Y):
        return coefs[k, X, pl.ds(Y, 1), :]

    def dcoef(X, Y):
        return ext[DD, X, pl.ds(Y, 1), :]

    for h in range(HALVES):
        @pl.loop(lo_x, hi_x)
        def _(X, h=h):
            for Y in range(lo_y, hi_y):
                t1[h, X, Y] = -(vp[h, X - lo_x + 1, Y - lo_y + 1] * coef(R0, X, Y))

    on(lambda k: landed0(k).wait_recv(), every)

    for f in range(4):
        for i in range(REACH):
            ext[f, i, pl.ds(lo_y, sy), :] = r0[0, 1 + f * REACH + i]
            ext[f, hi_x + i, pl.ds(lo_y, sy), :] = r0[1, 1 + f * REACH + i]
            for k, Y in ((2, i), (3, hi_y + i)):
                strip = r0[k, 1 + f * REACH + i]
                for x in range(sx):
                    ext[f, lo_x + x, Y:Y + 1, :] = strip[x:x + 1]
        for k in range(4, 8):
            dx, dy = NEIGHBOURS[k]
            for i in range(2):
                for j in range(2):
                    X, Y = (lo_x - 2 + i if dx < 0 else hi_x + i), (lo_y - 2 + j if dy < 0 else hi_y + j)
                    r = f * 4 + i * 2 + j
                    ext[f, X, Y:Y + 1, :] = r0[k, 1 + r // TILE, r % TILE:r % TILE + 1]

    layer = lax.broadcasted_iota(jnp.int32, (ey_n, layers), 1)
    first, last = layer == 0, layer == layers - 1

    def lift(f):
        return jnp.where(first, 0.0, pltpu.roll(f, 1, 1))

    def drop(f):
        return jnp.where(last, 0.0, pltpu.roll(f, layers - 1, 1))

    def next_conc(now, later, margin, tail=None):
        @pl.loop(margin, ex_n - margin)
        def _(X):
            c, d, u, w = ext[now, X], ext[DD, X], ext[UU, X], ext[WW, X]
            beside = (
                ext[now, X - 1] + ext[now, X + 1] + pltpu.roll(c, 1, 0) + pltpu.roll(c, ey_n - 1, 0)
                + lift(c) + drop(c)
            )
            carried = u * c
            new = c + d * (beside - 6.0 * c) + lift(carried) - carried - w * c / (HALF_SATURATION + c)
            ext[later, X] = new
            held = HALF_SATURATION + new
            coefs[R1 + later - C1, X] = new / held
            coefs[A1 + later - C1, X] = 1.0 - 6.0 * d - u - w * HALF_SATURATION / (held * held)

    next_conc(C0, C1, 1)
    next_conc(C1, C2, 2)
    next_conc(C2, C3, 3)

    for i in range(2):
        s3[0, i] = coefs[A3, lo_x + i, pl.ds(lo_y, sy), :]
        s3[1, i] = coefs[A3, hi_x - 2 + i, pl.ds(lo_y, sy), :]
        for k, Y in ((2, lo_y + i), (3, hi_y - 2 + i)):
            for x in range(sx):
                s3[k, i, x:x + 1] = coefs[A3, lo_x + x, Y:Y + 1, :]
    for k in range(4, 8):
        dx, dy = NEIGHBOURS[k]
        X, Y = (lo_x if dx < 0 else hi_x - 1), (lo_y if dy < 0 else hi_y - 1)
        s3[k, 0] = jnp.broadcast_to(coefs[A3, X, Y:Y + 1, :], (TILE, layers))
    on(lambda k: copy3(k).start(), every)
    on(lambda k: copy_v(1, k).start(), sides)

    @pl.loop(1, ex_n - 1)
    def _(X):
        d, u = ext[DD, X], ext[UU, X]
        coefs[DZ, X] = jnp.where(last, 0.0, d)
        coefs[BU, X] = jnp.where(first, 0.0, d) + lift(u)
        coefs[DL, X] = lift(d)
        coefs[DC, X] = drop(d) + jnp.where(last, 0.0, u)

    lane1 = lax.broadcasted_iota(jnp.int32, (1, layers), 1)
    keys, depths = {}, {}
    for k, b in enumerate(BLOCKS):
        tile = r0[k, 0] if k < 8 else s0[0, 0]
        low = place_of(b)[1] == 0
        keys[b] = jnp.where((lane1 < half_lanes) == low, tile[0:1], -1.0)
        depths[b] = tile[1:2]
    level = lax.broadcasted_iota(jnp.int32, (layers, layers), 0).astype(jnp.float32)
    for p in range(PAIRS):
        pair = BLOCKS[2 * p:2 * p + 2]
        where = jnp.where(lane1 < half_lanes, depths[pair[0]], depths[pair[-1]])
        hot = jnp.where(level == where, 1.0, 0.0).astype(jnp.bfloat16)
        zr[p, 0:layers] = hot
        zr[p, layers:2 * layers] = hot
        zi[p, :, 0:layers] = hot
        zi[p, :, layers:2 * layers] = hot
    yrow = lax.broadcasted_iota(jnp.int32, (ey_n, layers), 0)
    ymod = (yrow + (sy - REACH % sy)) % sy
    key_at = {
        dx: jnp.where(yrow < lo_y, keys[(dx, -1)], jnp.where(yrow < hi_y, keys[(dx, 0)], keys[(dx, 1)]))
        for dx in (-1, 0, 1)
    }
    for X in range(ex_n):
        dx = -1 if X < lo_x else 1 if X >= hi_x else 0
        name = (((X - REACH) % sx) * sy + ymod).astype(jnp.float32)
        for t in range(1, STEPS + 1):
            mark = jnp.where(key_at[dx] == name + float(cols * t), 1.0, 0.0)
            if t > 1:
                marks[t - 2, X] = mark
            elif dx == 0:
                ones[X - lo_x] = mark
    for t in range(1, STEPS + 1):
        mark = ones[...] if t == 1 else marks[t - 2, pl.ds(lo_x, sx)]
        count = lax.dot_general(
            mark.reshape(sx * ey_n, layers).astype(jnp.bfloat16), zi[PAIRS - 1, :, 0:layers],
            (((1,), (1,)), ((), ())), preferred_element_type=jnp.float32,
        )
        coefs[N1 + t - 1, pl.ds(lo_x, sx)] = count.reshape(sx, ey_n, layers)

    def up(f):
        return pltpu.roll(f, 1, 1)

    def down(f):
        return pltpu.roll(f, layers - 1, 1)

    def add(terms):
        return functools.reduce(lambda p, q: p + q, terms)

    def rows(reach, body):
        for X in range(lo_x, hi_x):
            body(X, 0, 0)
        for j in range(1, reach + 1):
            body(lo_x - j, j, 1)
            body(hi_x + j - 1, j, -1)

    def out_y(Y):
        return max(0, lo_y - Y, Y - hi_y + 1)

    def tangent_row(h, reach, prev, new, ka, kr, X, ex, inward):
        held = reach - 1
        mid = {}
        if ex <= held:
            mid = {Y: prev[h, X, Y] for Y in range(lo_y - held + ex, hi_y + held - ex)}
        for Y in range(lo_y - reach + ex, hi_y + reach - ex):
            ey = out_y(Y)
            terms = [mid[near] for near in (Y - 1, Y + 1) if near in mid]
            if ex == 0:
                if ey <= held:
                    terms += [prev[h, X - 1, Y], prev[h, X + 1, Y]]
            else:
                terms.append(prev[h, X + inward, Y])
                if ex + 1 + ey <= held:
                    terms.append(prev[h, X - inward, Y])
            value = dcoef(X, Y) * add(terms)
            if ex + ey < reach:
                p = mid[Y]
                value = (
                    value + coef(ka, X, Y) * p + coef(DZ, X, Y) * down(p) + coef(BU, X, Y) * up(p)
                )
                if ex == 0 and ey == 0:
                    value = value - coef(kr, X, Y) * vp[h, X - lo_x + 1, Y - lo_y + 1]
            new[h, X, Y] = value

    def block_of(X, Y):
        return (
            -1 if X < lo_x else 1 if X >= hi_x else 0,
            -1 if Y < lo_y else 1 if Y >= hi_y else 0,
        )

    def touched(p, reach):
        found = []
        for X in range(ex_n):
            for Y in range(lo_y + sy + REACH):
                b = block_of(X, Y)
                if place_of(b)[0] != p:
                    continue
                if b == OWN:
                    near = min(X - lo_x, hi_x - 1 - X, Y - lo_y, hi_y - 1 - Y) < reach
                else:
                    near = max(0, lo_x - X, X - hi_x + 1) + out_y(Y) <= reach
                if near:
                    found.append((X, Y))
        return found

    chunk = 16

    def read(h, p, wanted):
        total = None
        for start in range(0, len(wanted), chunk):
            some = wanted[start:start + chunk]
            high, low = [], []
            for field, t, X, Y in some:
                value = field[h, X, Y]
                top = value.astype(jnp.bfloat16)
                high.append(top)
                low.append((value - top.astype(jnp.float32)).astype(jnp.bfloat16))
            left = jnp.concatenate([jnp.concatenate(high, axis=0), jnp.concatenate(low, axis=0)], axis=1)
            got = lax.dot_general(left, zr[p], (((1,), (0,)), ((), ())), preferred_element_type=jnp.float32)
            for i, (field, t, X, Y) in enumerate(some):
                term = got[i * depth:(i + 1) * depth] * marks[t - 2, X, pl.ds(Y, 1), :]
                total = term if total is None else total + term
        return total

    @pl.loop(0, HALVES)
    def _(h):
        rows(1, functools.partial(tangent_row, h, 1, t1, t2, A1, R1))
        rows(2, functools.partial(tangent_row, h, 2, t2, t3, A2, R2))
        for p in range(PAIRS):
            acc[h, p] = read(
                h, p, [(t2, 2, *at) for at in touched(p, 1)] + [(t3, 3, *at) for at in touched(p, 2)]
            )

    on(lambda k: landed3(k).wait_recv(), every)
    for i in range(2):
        coefs[A3, lo_x - 2 + i, pl.ds(lo_y, sy), :] = r3[0, i]
        coefs[A3, hi_x + i, pl.ds(lo_y, sy), :] = r3[1, i]
        for k, Y in ((2, lo_y - 2 + i), (3, hi_y + i)):
            for x in range(sx):
                coefs[A3, lo_x + x, Y:Y + 1, :] = r3[k, i, x:x + 1]
    for k in range(4, 8):
        dx, dy = NEIGHBOURS[k]
        X, Y = (lo_x - 1 if dx < 0 else hi_x), (lo_y - 1 if dy < 0 else hi_y)
        coefs[A3, X, Y:Y + 1, :] = r3[k, 0, 0:1]

    lane = lax.broadcasted_iota(jnp.int32, (depth, layers), 1)
    lower = lane < half_lanes

    def moved(value, source, target):
        return value if source == target else pltpu.roll(value, half_lanes, 1)

    @pl.loop(0, HALVES)
    def _(h):
        rows(3, functools.partial(tangent_row, h, 3, t3, t4, A3, R3))
        mine = []
        for p in range(PAIRS):
            mine.append(acc[h, p] + read(h, p, [(t4, 4, *at) for at in touched(p, 3)]))
            part[h, p] = mine[p]
        for k, d in enumerate(NEIGHBOURS):
            need = shared(d)
            for j in range(0, len(need), 2):
                (pa, ha), (pb, hb) = place_of(need[j]), place_of(need[j + 1])
                s1[h, k, j // 2] = jnp.where(lower, moved(mine[pa], ha, 0), moved(mine[pb], hb, 1))
        on(lambda k: copy1(h, k).start(), every)

    for h in range(HALVES):
        on(lambda k: landed_v(h, k).wait_recv(), sides)
    not_first = jnp.where(lane1 == 0, 0.0, 1.0)
    not_last = jnp.where(lane1 == layers - 1, 0.0, 1.0)

    @pl.loop(0, HALVES)
    def _(h):
        for x in range(sx):
            X = x + lo_x
            mid = [vp[h, x + 1, y] for y in range(sy + 2)]
            for y in range(sy):
                Y = y + lo_y
                v = mid[y + 1]
                beside = (
                    (vp[h, x, y + 1] + vp[h, x + 2, y + 1]) + (mid[y] + mid[y + 2])
                    + not_first * up(v) + not_last * down(v)
                )
                first_sensors = coef(R0, X, Y) * (coef(N1, X, Y) * t1[h, X, Y])
                out[x * sy + y, pl.ds(h * depth, depth)] = (
                    PRIOR_WEIGHT * ((6.0 + PRIOR_SHIFT) * v - beside) - first_sensors
                )

    def inject(p, t, reach, use):
        wanted = touched(p, reach)
        for start in range(0, len(wanted), chunk):
            some = wanted[start:start + chunk]
            high, low = [], []
            for X, Y in some:
                mark = jnp.broadcast_to(marks[t - 2, X, pl.ds(Y, 1), :], (depth, layers)).astype(jnp.bfloat16)
                high.append(ysplit[p, 0] * mark)
                low.append(ysplit[p, 1] * mark)
            left = jnp.concatenate([jnp.concatenate(high, axis=0), jnp.concatenate(low, axis=0)], axis=1)
            got = lax.dot_general(left, zi[p], (((1,), (1,)), ((), ())), preferred_element_type=jnp.float32)
            for i, (X, Y) in enumerate(some):
                use(X, Y, got[i * depth:(i + 1) * depth])

    def adjoint(hold, q, ka, X, Y, centre):
        a = hold[X, Y] if centre is None else centre
        return (
            coef(ka, X, Y) * a
            + ((q[X - 1, Y] + q[X + 1, Y]) + (q[X, Y - 1] + q[X, Y + 1]))
            + coef(DL, X, Y) * up(a)
            + coef(DC, X, Y) * down(a)
        )

    def adjoint_row(h, reach, hold, q, new_hold, new_q, placed, tangent, ka, kn, X, ex, inward):
        for Y in range(lo_y - reach + ex, hi_y + reach - ex):
            a = adjoint(hold, q, ka, X, Y, None) + placed[X, Y]
            if ex == 0 and out_y(Y) == 0:
                a = a + coef(kn, X, Y) * tangent[h, X, Y]
            new_hold[X, Y] = a
            new_q[X, Y] = dcoef(X, Y) * a

    inner = [
        (X, Y) for X in range(lo_x, hi_x) for Y in range(lo_y, hi_y) if (X, Y) not in touched(PAIRS - 1, 3)
    ]

    @pl.loop(0, HALVES)
    def _(h):
        on(lambda k: landed1(h, k).wait_recv(), every)
        total = [part[h, p] for p in range(PAIRS - 1)] + [blank]
        for k, d in enumerate(NEIGHBOURS):
            need = shared(NEIGHBOURS[k ^ 1])
            for j, b in enumerate(need):
                p, target = place_of((b[0] + d[0], b[1] + d[1]))
                value = moved(r1[h, k, j // 2], j % 2, target)
                total[p] = total[p] + jnp.where(lower == (target == 0), value, 0.0)
        for p in range(PAIRS):
            top = total[p].astype(jnp.bfloat16)
            ysplit[p, 0] = top
            ysplit[p, 1] = (total[p] - top.astype(jnp.float32)).astype(jnp.bfloat16)

        def last_step(X, Y, value):
            a4[X, Y] = value
            q4[X, Y] = dcoef(X, Y) * value

        def last_own(X, Y, value):
            last_step(X, Y, value + coef(N4, X, Y) * t4[h, X, Y])

        def to_three(X, Y, value):
            pl3[X, Y] = value

        def to_two(X, Y, value):
            pl2[X, Y] = value

        for p in range(PAIRS):
            inject(p, 4, 3, last_own if p == PAIRS - 1 else last_step)
            inject(p, 3, 2, to_three)
            inject(p, 2, 1, to_two)
        for X, Y in inner:
            last_step(X, Y, coef(N4, X, Y) * t4[h, X, Y])
        rows(2, functools.partial(adjoint_row, h, 2, a4, q4, a3, q3, pl3, t3, A3, N3))
        rows(1, functools.partial(adjoint_row, h, 1, a3, q3, a2, q2, pl2, t2, A2, N2))

        for x in range(sx):
            X = x + lo_x
            for y in range(sy):
                Y = y + lo_y
                middle = a2[X, Y]
                gradient = (
                    coef(R3, X, Y) * a4[X, Y] + coef(R2, X, Y) * a3[X, Y] + coef(R1, X, Y) * middle
                    + coef(R0, X, Y) * adjoint(a2, q2, A1, X, Y, middle)
                )
                at = (x * sy + y, pl.ds(h * depth, depth))
                out[at] = out[at] - gradient

    on(lambda k: copy0(k).wait_send(), every)
    on(lambda k: copy3(k).wait_send(), every)
    for h in range(HALVES):
        on(lambda k: copy_v(h, k).wait_send(), sides)
        on(lambda k: copy1(h, k).wait_send(), every)


def on_device(conc_start, diffusion, courant, uptake, directions, sensor_cell, sensor_step):
    count_dir, sx, sy, layers = directions.shape
    depth = count_dir // HALVES
    sensors = sensor_cell.shape[-1]
    assert sensors <= layers // 2 and min(sx, sy) >= 2 * REACH and depth % 16 == 0
    ex_n, ey_n = sx + 2 * REACH, pl.cdiv(sy + 2 * REACH, TILE) * TILE
    vmem = pltpu.VMEM
    wide = sy + 2 * REACH
    both = vmem((HALVES, ex_n, wide, depth, layers), jnp.float32)
    one = vmem((ex_n, wide, depth, layers), jnp.float32)

    def table(n):
        return vmem((n, ex_n, ey_n, layers), jnp.float32)

    tiles = 1 + 4 * REACH
    sems = pltpu.SemaphoreType.DMA
    result = pl.pallas_call(
        functools.partial(kernel, sx, sy, depth),
        out_shape=jax.ShapeDtypeStruct((sx * sy, count_dir, layers), jnp.float32),
        in_specs=[pl.BlockSpec(memory_space=vmem)] * 7,
        out_specs=pl.BlockSpec(memory_space=vmem),
        scratch_shapes=[
            vmem((HALVES, sx + 2, sy + 2, depth, layers), jnp.float32),
            *[both] * 4,
            *[one] * 8,
            table(7),
            table(15),
            table(STEPS - 1),
            vmem((sx, ey_n, layers), jnp.float32),
            vmem((TILE, layers), jnp.int32),
            vmem((PAIRS, 2 * layers, layers), jnp.bfloat16),
            vmem((PAIRS, layers, 2 * layers), jnp.bfloat16),
            vmem((HALVES, PAIRS, depth, layers), jnp.float32),
            vmem((HALVES, PAIRS, depth, layers), jnp.float32),
            vmem((PAIRS, 2, depth, layers), jnp.bfloat16),
            vmem((8, tiles, TILE, layers), jnp.float32),
            vmem((8, tiles, TILE, layers), jnp.float32),
            vmem((8, 2, TILE, layers), jnp.float32),
            vmem((8, 2, TILE, layers), jnp.float32),
            vmem((HALVES, 8, 3, depth, layers), jnp.float32),
            vmem((HALVES, 8, 3, depth, layers), jnp.float32),
            sems((8,)), sems((8,)),
            sems((8,)), sems((8,)),
            sems((HALVES, 4)), sems((HALVES, 4)),
            sems((HALVES, 8)), sems((HALVES, 8)),
        ],
        compiler_params=pltpu.CompilerParams(
            collective_id=0, has_side_effects=True, vmem_limit_bytes=56 * 2**20
        ),
    )(
        conc_start, diffusion, courant, uptake,
        directions.reshape(count_dir * sx * sy, layers),
        sensor_cell.reshape(1, sensors), sensor_step.reshape(1, sensors),
    )
    return jnp.swapaxes(result, 0, 1).reshape(count_dir, sx, sy, layers)


def solution(mesh):
    in_specs = (
        P("gx", "gy", None),
        P("gx", "gy", None),
        P("gx", "gy", None),
        P("gx", "gy", None),
        P(None, "gx", "gy", None),
        P("gx", "gy", None),
        P("gx", "gy", None),
    )
    out_specs = P(None, "gx", "gy", None)
    return jax.shard_map(
        on_device, mesh=mesh, in_specs=in_specs, out_specs=out_specs, check_vma=False
    )
```

```python
import functools

import jax
import jax.numpy as jnp
from jax import lax
from jax.experimental import pallas as pl
from jax.experimental.pallas import tpu as pltpu
from jax.sharding import PartitionSpec as P

STEPS = 4
REACH = STEPS - 1
HALF_SATURATION = 0.5
PRIOR_WEIGHT = 0.2
PRIOR_SHIFT = 0.5
HALVES = 2
TILE = 8

MESH = pl.DeviceIdType.MESH

NEIGHBOURS = ((-1, 0), (1, 0), (0, -1), (0, 1), (-1, -1), (1, 1), (-1, 1), (1, -1))
OWN = (0, 0)
BLOCKS = (*NEIGHBOURS, OWN)
PAIRS = 5

A1, A2, A3, DZ, BU, DL, DC, R0, R1, R2, R3, N1, N2, N3, N4 = range(15)
C0, DD, UU, WW, C1, C2, C3 = range(7)


WIDTHS = (3, 3, 2, 2)
CORNERS = ((1, 1), (1, 2), (2, 1))


def place_of(block):
    k = BLOCKS.index(block)
    return (k // 2, k % 2)


def corner_cells(f):
    base = sum(w * (w - 1) // 2 for w in WIDTHS[:f])
    return [(i, j, base + r) for r, (i, j) in enumerate(CORNERS[:WIDTHS[f] * (WIDTHS[f] - 1) // 2])]


def shared(d):
    return [b for b in BLOCKS if abs(b[0] - d[0]) <= 1 and abs(b[1] - d[1]) <= 1]


def kernel(
    sx, sy, depth,
    conc, diffusion, courant, uptake, dirs_in, cells, when, out,
    dirs, result, marked,
    vp, t1, t2, t3, t4, a4, a3, a2, q4, q3, q2, pl3, pl2,
    ext, coefs, marks, ones, ii, zr, zi, acc, part, ysplit,
    s0, r0, s3, r3, s1, r1,
    in_sem, out_sem,
    s0_send, s0_recv, s3_send, s3_recv, v_send, v_recv, s1_send, s1_recv,
):
    layers = conc.shape[-1]
    fetch = pltpu.make_async_copy(dirs_in, dirs, in_sem)
    fetch.start()
    half_lanes = layers // 2
    cols = sx * sy
    ex_n, ey_n = ext.shape[1], ext.shape[2]
    lo_x, hi_x, lo_y, hi_y = REACH, REACH + sx, REACH, REACH + sy
    ix, iy = lax.axis_index("gx"), lax.axis_index("gy")
    nx, ny = lax.axis_size("gx"), lax.axis_size("gy")
    have, partner = [], []
    for dx, dy in NEIGHBOURS:
        here = []
        if dx:
            here.append(ix > 0 if dx < 0 else ix < nx - 1)
        if dy:
            here.append(iy > 0 if dy < 0 else iy < ny - 1)
        have.append(functools.reduce(jnp.logical_and, here))
        px = jnp.maximum(ix - 1, 0) if dx < 0 else jnp.minimum(ix + 1, nx - 1) if dx > 0 else ix
        py = jnp.maximum(iy - 1, 0) if dy < 0 else jnp.minimum(iy + 1, ny - 1) if dy > 0 else iy
        partner.append((px, py))
    sides = range(4)
    every = range(8)

    def on(action, ks):
        for k in ks:
            @pl.when(have[k])
            def _(k=k):
                action(k)

    barrier = pltpu.get_barrier_semaphore()
    on(lambda k: pl.semaphore_signal(barrier, inc=1, device_id=partner[k], device_id_type=MESH), every)

    def remote(src, dst, send, recv, k):
        return pltpu.make_async_remote_copy(
            src_ref=src, dst_ref=dst, send_sem=send, recv_sem=recv, device_id=partner[k], device_id_type=MESH
        )

    def size0(k):
        return 1 + sum(WIDTHS) if k < 4 else 2

    def copy0(k):
        n = pl.ds(0, size0(k))
        return remote(s0.at[k, n], r0.at[k ^ 1, n], s0_send.at[k], s0_recv.at[k ^ 1], k)

    def landed0(k):
        n = pl.ds(0, size0(k))
        return remote(r0.at[k, n], r0.at[k, n], s0_send.at[k], s0_recv.at[k], k)

    def size3(k):
        return 2 if k < 4 else 1

    def copy3(k):
        n = pl.ds(0, size3(k))
        return remote(s3.at[k, n], r3.at[k ^ 1, n], s3_send.at[k], s3_recv.at[k ^ 1], k)

    def landed3(k):
        n = pl.ds(0, size3(k))
        return remote(r3.at[k, n], r3.at[k, n], s3_send.at[k], s3_recv.at[k], k)

    def v_at(h, k, halo):
        if k == 0:
            return vp.at[h, 0 if halo else 1, pl.ds(1, sy)]
        if k == 1:
            return vp.at[h, sx + 1 if halo else sx, pl.ds(1, sy)]
        if k == 2:
            return vp.at[h, pl.ds(1, sx), 0 if halo else 1]
        return vp.at[h, pl.ds(1, sx), sy + 1 if halo else sy]

    def copy_v(h, k):
        return remote(v_at(h, k, False), v_at(h, k ^ 1, True), v_send.at[h, k], v_recv.at[h, k ^ 1], k)

    def landed_v(h, k):
        return remote(v_at(h, k, True), v_at(h, k, True), v_send.at[h, k], v_recv.at[h, k], k)

    def size1(k):
        return (len(shared(NEIGHBOURS[k])) + 1) // 2

    def copy1(h, k):
        n = pl.ds(0, size1(k))
        return remote(s1.at[h, k, n], r1.at[h, k ^ 1, n], s1_send.at[h, k], s1_recv.at[h, k ^ 1], k)

    def landed1(h, k):
        n = pl.ds(0, size1(k))
        return remote(r1.at[h, k, n], r1.at[h, k, n], s1_send.at[h, k], s1_recv.at[h, k], k)

    fields = (conc, diffusion, courant, uptake)
    sensors = cells.shape[1]
    ii[...] = jnp.full(ii.shape, -1, jnp.int32)
    ii[0:1, 0:sensors] = cells[...] // layers + cols * when[...]
    ii[1:2, 0:sensors] = cells[...] % layers
    lane8 = lax.broadcasted_iota(jnp.int32, ii.shape, 1)
    packed = ii[...]
    about = jnp.where(lane8 < half_lanes, packed, pltpu.roll(packed, half_lanes, 1)).astype(jnp.float32)
    for k in every:
        s0[k, 0] = about
    for f, field in enumerate(fields):
        block = field[...]
        base, width = 1 + sum(WIDTHS[:f]), WIDTHS[f]
        for i in range(width):
            s0[0, base + i] = block[i]
            s0[1, base + i] = block[sx - width + i]
            for k, y in ((2, i), (3, sy - width + i)):
                s0[k, base + i] = jnp.concatenate([block[x, y:y + 1] for x in range(sx)], axis=0)
        for k in range(4, 8):
            dx, dy = NEIGHBOURS[k]
            for i, j, r in corner_cells(f):
                x, y = (i - 1 if dx < 0 else sx - i), (j - 1 if dy < 0 else sy - j)
                s0[k, 1, r:r + 1] = block[x, y:y + 1]

    pl.semaphore_wait(barrier, sum(jnp.where(here, 1, 0) for here in have))
    on(lambda k: copy0(k).start(), every)

    fetch.wait()
    for h in range(HALVES):
        @pl.loop(0, sx)
        def _(x, h=h):
            for y in range(sy):
                vp[h, x + 1, y + 1] = dirs[pl.ds(h * depth * cols + x * sy + y, depth, stride=cols), :]

    for k in every:
        @pl.when(jnp.logical_not(have[k]))
        def _(k=k):
            r0[k] = jnp.zeros(r0.shape[1:], jnp.float32)
            r3[k] = jnp.zeros(r3.shape[1:], jnp.float32)
            for h in range(HALVES):
                if k < 4:
                    r1[h, k] = jnp.zeros(r1.shape[2:], jnp.float32)
                    ref = v_at(h, k, True)
                    ref[...] = jnp.zeros(ref.shape, jnp.float32)

    blank = jnp.zeros((depth, layers), jnp.float32)
    for h in range(HALVES):
        for X in (lo_x - 1, hi_x):
            for Y in range(lo_y, hi_y):
                t1[h, X, Y] = blank
            for Y in (lo_y - 1, hi_y):
                t2[h, X, Y] = blank
            for Y in (lo_y - 2, hi_y + 1):
                t3[h, X, Y] = blank
    for X in range(lo_x, hi_x):
        for Y in range(lo_y, hi_y):
            pl3[X, Y] = blank
            pl2[X, Y] = blank
    for f in range(4):
        ext[f] = jnp.zeros(ext.shape[1:], jnp.float32)
    for k in (A1, A2, A3):
        coefs[k] = jnp.zeros(coefs.shape[1:], jnp.float32)
    for f, field in enumerate(fields):
        for x in range(sx):
            ext[f, lo_x + x, pl.ds(lo_y, sy), :] = field[x]

    for X in range(lo_x, hi_x):
        c = ext[C0, X]
        coefs[R0, X] = c / (HALF_SATURATION + c)

    def coef(k, X, Y):
        return coefs[k, X, pl.ds(Y, 1), :]

    def dcoef(X, Y):
        return ext[DD, X, pl.ds(Y, 1), :]

    for h in range(HALVES):
        @pl.loop(lo_x, hi_x)
        def _(X, h=h):
            for Y in range(lo_y, hi_y):
                t1[h, X, Y] = -(vp[h, X - lo_x + 1, Y - lo_y + 1] * coef(R0, X, Y))

    on(lambda k: landed0(k).wait_recv(), every)

    for f in range(4):
        base, width = 1 + sum(WIDTHS[:f]), WIDTHS[f]
        for i in range(width):
            ext[f, lo_x - width + i, pl.ds(lo_y, sy), :] = r0[0, base + i]
            ext[f, hi_x + i, pl.ds(lo_y, sy), :] = r0[1, base + i]
            for k, Y in ((2, lo_y - width + i), (3, hi_y + i)):
                strip = r0[k, base + i]
                for x in range(sx):
                    ext[f, lo_x + x, Y:Y + 1, :] = strip[x:x + 1]
        for k in range(4, 8):
            dx, dy = NEIGHBOURS[k]
            for i, j, r in corner_cells(f):
                X, Y = (lo_x - i if dx < 0 else hi_x + i - 1), (lo_y - j if dy < 0 else hi_y + j - 1)
                ext[f, X, Y:Y + 1, :] = r0[k, 1, r:r + 1]

    layer = lax.broadcasted_iota(jnp.int32, (ey_n, layers), 1)
    first, last = layer == 0, layer == layers - 1

    def lift(f):
        return jnp.where(first, 0.0, pltpu.roll(f, 1, 1))

    def drop(f):
        return jnp.where(last, 0.0, pltpu.roll(f, layers - 1, 1))

    def next_conc(now, later, margin, tail=None):
        for X in range(margin, ex_n - margin):
            c, d, u, w = ext[now, X], ext[DD, X], ext[UU, X], ext[WW, X]
            beside = (
                ext[now, X - 1] + ext[now, X + 1] + pltpu.roll(c, 1, 0) + pltpu.roll(c, ey_n - 1, 0)
                + lift(c) + drop(c)
            )
            carried = u * c
            new = c + d * (beside - 6.0 * c) + lift(carried) - carried - w * c / (HALF_SATURATION + c)
            ext[later, X] = new
            held = HALF_SATURATION + new
            coefs[R1 + later - C1, X] = new / held
            coefs[A1 + later - C1, X] = 1.0 - 6.0 * d - u - w * HALF_SATURATION / (held * held)

    next_conc(C0, C1, 1)
    next_conc(C1, C2, 2)
    next_conc(C2, C3, 3)

    for i in range(2):
        s3[0, i] = coefs[A3, lo_x + i, pl.ds(lo_y, sy), :]
        s3[1, i] = coefs[A3, hi_x - 2 + i, pl.ds(lo_y, sy), :]
        for k, Y in ((2, lo_y + i), (3, hi_y - 2 + i)):
            for x in range(sx):
                s3[k, i, x:x + 1] = coefs[A3, lo_x + x, Y:Y + 1, :]
    for k in range(4, 8):
        dx, dy = NEIGHBOURS[k]
        X, Y = (lo_x if dx < 0 else hi_x - 1), (lo_y if dy < 0 else hi_y - 1)
        s3[k, 0] = jnp.broadcast_to(coefs[A3, X, Y:Y + 1, :], (TILE, layers))
    on(lambda k: copy3(k).start(), every)
    for h in range(HALVES):
        on(lambda k: copy_v(h, k).start(), sides)

    for X in range(1, ex_n - 1):
        d, u = ext[DD, X], ext[UU, X]
        coefs[DZ, X] = jnp.where(last, 0.0, d)
        coefs[BU, X] = jnp.where(first, 0.0, d) + lift(u)
        coefs[DL, X] = lift(d)
        coefs[DC, X] = drop(d) + jnp.where(last, 0.0, u)

    lane1 = lax.broadcasted_iota(jnp.int32, (1, layers), 1)
    keys, depths = {}, {}
    for k, b in enumerate(BLOCKS):
        tile = r0[k, 0] if k < 8 else s0[0, 0]
        low = place_of(b)[1] == 0
        keys[b] = jnp.where((lane1 < half_lanes) == low, tile[0:1], -1.0)
        depths[b] = tile[1:2]
    level = lax.broadcasted_iota(jnp.int32, (layers, layers), 0).astype(jnp.float32)
    for p in range(PAIRS):
        pair = BLOCKS[2 * p:2 * p + 2]
        where = jnp.where(lane1 < half_lanes, depths[pair[0]], depths[pair[-1]])
        hot = jnp.where(level == where, 1.0, 0.0).astype(jnp.bfloat16)
        zr[p, 0:layers] = hot
        zr[p, layers:2 * layers] = hot
        zi[p, :, 0:layers] = hot
        zi[p, :, layers:2 * layers] = hot
    yrow = lax.broadcasted_iota(jnp.int32, (ey_n, layers), 0)
    ymod = (yrow + (sy - REACH % sy)) % sy
    key_at = {
        dx: jnp.where(yrow < lo_y, keys[(dx, -1)], jnp.where(yrow < hi_y, keys[(dx, 0)], keys[(dx, 1)]))
        for dx in (-1, 0, 1)
    }
    for X in range(ex_n):
        dx = -1 if X < lo_x else 1 if X >= hi_x else 0
        name = (((X - REACH) % sx) * sy + ymod).astype(jnp.float32)
        for t in range(1, STEPS + 1):
            mark = jnp.where(key_at[dx] == name + float(cols * t), 1.0, 0.0)
            if t > 1:
                marks[t - 2, X] = mark
            elif dx == 0:
                ones[X - lo_x] = mark
    for t in range(1, STEPS + 1):
        mark = ones[...] if t == 1 else marks[t - 2, pl.ds(lo_x, sx)]
        count = lax.dot_general(
            mark.reshape(sx * ey_n, layers).astype(jnp.bfloat16), zi[PAIRS - 1, :, 0:layers],
            (((1,), (1,)), ((), ())), preferred_element_type=jnp.float32,
        )
        coefs[N1 + t - 1, pl.ds(lo_x, sx)] = count.reshape(sx, ey_n, layers)

    def up(f):
        return pltpu.roll(f, 1, 1)

    def down(f):
        return pltpu.roll(f, layers - 1, 1)

    def add(terms):
        return functools.reduce(lambda p, q: p + q, terms)

    def rows(reach, body):
        for X in range(lo_x, hi_x):
            body(X, 0, 0)
        for j in range(1, reach + 1):
            body(lo_x - j, j, 1)
            body(hi_x + j - 1, j, -1)

    def out_y(Y):
        return max(0, lo_y - Y, Y - hi_y + 1)

    def tangent_row(h, reach, prev, new, ka, kr, X, ex, inward):
        held = reach - 1
        mid = {}
        if ex <= held:
            mid = {Y: prev[h, X, Y] for Y in range(lo_y - held + ex, hi_y + held - ex)}
        for Y in range(lo_y - reach + ex, hi_y + reach - ex):
            ey = out_y(Y)
            terms = [mid[near] for near in (Y - 1, Y + 1) if near in mid]
            if ex == 0:
                if ey <= held:
                    terms += [prev[h, X - 1, Y], prev[h, X + 1, Y]]
            else:
                terms.append(prev[h, X + inward, Y])
                if ex + 1 + ey <= held:
                    terms.append(prev[h, X - inward, Y])
            value = dcoef(X, Y) * add(terms)
            if ex + ey < reach:
                p = mid[Y]
                value = (
                    value + coef(ka, X, Y) * p + coef(DZ, X, Y) * down(p) + coef(BU, X, Y) * up(p)
                )
                if ex == 0 and ey == 0:
                    value = value - coef(kr, X, Y) * vp[h, X - lo_x + 1, Y - lo_y + 1]
            new[h, X, Y] = value

    def block_of(X, Y):
        return (
            -1 if X < lo_x else 1 if X >= hi_x else 0,
            -1 if Y < lo_y else 1 if Y >= hi_y else 0,
        )

    def touched(p, reach):
        found = []
        for X in range(ex_n):
            for Y in range(lo_y + sy + REACH):
                b = block_of(X, Y)
                if place_of(b)[0] != p:
                    continue
                if b == OWN:
                    near = min(X - lo_x, hi_x - 1 - X, Y - lo_y, hi_y - 1 - Y) < reach
                else:
                    near = max(0, lo_x - X, X - hi_x + 1) + out_y(Y) <= reach
                if near:
                    found.append((X, Y))
        return found

    chunk = 16

    def read(h, p, wanted):
        total = None
        for start in range(0, len(wanted), chunk):
            some = wanted[start:start + chunk]
            high, low = [], []
            for field, t, X, Y in some:
                value = field[h, X, Y]
                top = value.astype(jnp.bfloat16)
                high.append(top)
                low.append((value - top.astype(jnp.float32)).astype(jnp.bfloat16))
            left = jnp.concatenate([jnp.concatenate(high, axis=0), jnp.concatenate(low, axis=0)], axis=1)
            got = lax.dot_general(left, zr[p], (((1,), (0,)), ((), ())), preferred_element_type=jnp.float32)
            for i, (field, t, X, Y) in enumerate(some):
                term = got[i * depth:(i + 1) * depth] * marks[t - 2, X, pl.ds(Y, 1), :]
                total = term if total is None else total + term
        return total

    @pl.loop(0, HALVES)
    def _(h):
        rows(1, functools.partial(tangent_row, h, 1, t1, t2, A1, R1))
        rows(2, functools.partial(tangent_row, h, 2, t2, t3, A2, R2))
        for p in range(PAIRS):
            acc[h, p] = read(
                h, p, [(t2, 2, *at) for at in touched(p, 1)] + [(t3, 3, *at) for at in touched(p, 2)]
            )

    on(lambda k: landed3(k).wait_recv(), every)
    for i in range(2):
        coefs[A3, lo_x - 2 + i, pl.ds(lo_y, sy), :] = r3[0, i]
        coefs[A3, hi_x + i, pl.ds(lo_y, sy), :] = r3[1, i]
        for k, Y in ((2, lo_y - 2 + i), (3, hi_y + i)):
            for x in range(sx):
                coefs[A3, lo_x + x, Y:Y + 1, :] = r3[k, i, x:x + 1]
    for k in range(4, 8):
        dx, dy = NEIGHBOURS[k]
        X, Y = (lo_x - 1 if dx < 0 else hi_x), (lo_y - 1 if dy < 0 else hi_y)
        coefs[A3, X, Y:Y + 1, :] = r3[k, 0, 0:1]

    lane = lax.broadcasted_iota(jnp.int32, (depth, layers), 1)
    lower = lane < half_lanes

    def moved(value, source, target):
        return value if source == target else pltpu.roll(value, half_lanes, 1)

    def send_sums(h, sums, ks):
        for k in ks:
            need = shared(NEIGHBOURS[k])
            for j in range(0, len(need), 2):
                (pa, ha), (pb, hb) = place_of(need[j]), place_of(need[j + 1])
                s1[h, k, j // 2] = jnp.where(lower, moved(sums[pa], ha, 0), moved(sums[pb], hb, 1))
        on(lambda k: copy1(h, k).start(), ks)

    def add_sums(h, sums, ks):
        on(lambda k: landed1(h, k).wait_recv(), ks)
        for k in ks:
            d, need = NEIGHBOURS[k], shared(NEIGHBOURS[k ^ 1])
            for j, b in enumerate(need):
                p, target = place_of((b[0] + d[0], b[1] + d[1]))
                value = moved(r1[h, k, j // 2], j % 2, target)
                sums[p] = sums[p] + jnp.where(lower == (target == 0), value, 0.0)
        return sums

    def relay(h):
        sums = add_sums(h, [part[h, p] for p in range(PAIRS - 1)] + [blank], (2, 3))
        own = part[h, PAIRS - 1]
        for p in range(PAIRS):
            part[h, p] = sums[p]
        send_sums(h, sums[:-1] + [sums[-1] + own], (0, 1))

    @pl.loop(0, HALVES)
    def _(h):
        rows(3, functools.partial(tangent_row, h, 3, t3, t4, A3, R3))
        mine = []
        for p in range(PAIRS):
            mine.append(acc[h, p] + read(h, p, [(t4, 4, *at) for at in touched(p, 3)]))
            part[h, p] = mine[p]
        send_sums(h, mine, (2, 3))

    not_first = jnp.where(lane1 == 0, 0.0, 1.0)
    not_last = jnp.where(lane1 == layers - 1, 0.0, 1.0)

    def prior(h):
        on(lambda k: landed_v(h, k).wait_recv(), sides)
        for x in range(sx):
            X = x + lo_x
            mid = [vp[h, x + 1, y] for y in range(sy + 2)]
            for y in range(sy):
                Y = y + lo_y
                v = mid[y + 1]
                beside = (
                    (vp[h, x, y + 1] + vp[h, x + 2, y + 1]) + (mid[y] + mid[y + 2])
                    + not_first * up(v) + not_last * down(v)
                )
                first_sensors = coef(R0, X, Y) * (coef(N1, X, Y) * t1[h, X, Y])
                result[h, x * sy + y] = (
                    PRIOR_WEIGHT * ((6.0 + PRIOR_SHIFT) * v - beside) - first_sensors
                )

    for h in range(HALVES):
        prior(h)
        relay(h)

    for p in range(PAIRS):
        for t in range(2, STEPS + 1):
            for X, Y in touched(p, t - 1):
                mark = jnp.broadcast_to(marks[t - 2, X, pl.ds(Y, 1), :], (depth, layers))
                marked[t - 2, X, Y] = mark.astype(jnp.bfloat16)

    def inject(p, t, reach, use):
        wanted = touched(p, reach)
        for start in range(0, len(wanted), chunk):
            some = wanted[start:start + chunk]
            high, low = [], []
            for X, Y in some:
                mark = marked[t - 2, X, Y]
                high.append(ysplit[p, 0] * mark)
                low.append(ysplit[p, 1] * mark)
            left = jnp.concatenate([jnp.concatenate(high, axis=0), jnp.concatenate(low, axis=0)], axis=1)
            got = lax.dot_general(left, zi[p], (((1,), (1,)), ((), ())), preferred_element_type=jnp.float32)
            for i, (X, Y) in enumerate(some):
                use(X, Y, got[i * depth:(i + 1) * depth])

    def adjoint(hold, q, ka, X, Y, centre):
        a = hold[X, Y] if centre is None else centre
        return (
            coef(ka, X, Y) * a
            + ((q[X - 1, Y] + q[X + 1, Y]) + (q[X, Y - 1] + q[X, Y + 1]))
            + coef(DL, X, Y) * up(a)
            + coef(DC, X, Y) * down(a)
        )

    def adjoint_row(h, reach, hold, q, new_hold, new_q, placed, tangent, ka, kn, X, ex, inward):
        for Y in range(lo_y - reach + ex, hi_y + reach - ex):
            a = adjoint(hold, q, ka, X, Y, None) + placed[X, Y]
            if ex == 0 and out_y(Y) == 0:
                a = a + coef(kn, X, Y) * tangent[h, X, Y]
            new_hold[X, Y] = a
            new_q[X, Y] = dcoef(X, Y) * a

    inner = [
        (X, Y) for X in range(lo_x, hi_x) for Y in range(lo_y, hi_y) if (X, Y) not in touched(PAIRS - 1, 3)
    ]

    @pl.loop(0, HALVES)
    def _(h):
        total = add_sums(h, [part[h, p] for p in range(PAIRS)], (0, 1))
        for p in range(PAIRS):
            top = total[p].astype(jnp.bfloat16)
            ysplit[p, 0] = top
            ysplit[p, 1] = (total[p] - top.astype(jnp.float32)).astype(jnp.bfloat16)

        def last_step(X, Y, value):
            a4[X, Y] = value
            q4[X, Y] = dcoef(X, Y) * value

        def last_own(X, Y, value):
            last_step(X, Y, value + coef(N4, X, Y) * t4[h, X, Y])

        def to_three(X, Y, value):
            pl3[X, Y] = value

        def to_two(X, Y, value):
            pl2[X, Y] = value

        for p in range(PAIRS):
            inject(p, 4, 3, last_own if p == PAIRS - 1 else last_step)
            inject(p, 3, 2, to_three)
            inject(p, 2, 1, to_two)
        for X, Y in inner:
            last_step(X, Y, coef(N4, X, Y) * t4[h, X, Y])
        rows(2, functools.partial(adjoint_row, h, 2, a4, q4, a3, q3, pl3, t3, A3, N3))
        rows(1, functools.partial(adjoint_row, h, 1, a3, q3, a2, q2, pl2, t2, A2, N2))

        for x in range(sx):
            X = x + lo_x
            for y in range(sy):
                Y = y + lo_y
                middle = a2[X, Y]
                gradient = (
                    coef(R3, X, Y) * a4[X, Y] + coef(R2, X, Y) * a3[X, Y] + coef(R1, X, Y) * middle
                    + coef(R0, X, Y) * adjoint(a2, q2, A1, X, Y, middle)
                )
                at = x * sy + y
                result[h, at] = result[h, at] - gradient
                pltpu.make_async_copy(
                    result.at[h, at], out.at[pl.ds(h * depth, depth), at], out_sem.at[h]
                ).start()

    for h in range(HALVES):
        pltpu.make_async_copy(result.at[h], result.at[h], out_sem.at[h]).wait()
    on(lambda k: copy0(k).wait_send(), every)
    on(lambda k: copy3(k).wait_send(), every)
    for h in range(HALVES):
        on(lambda k: copy_v(h, k).wait_send(), sides)
        on(lambda k: copy1(h, k).wait_send(), sides)


def on_device(conc_start, diffusion, courant, uptake, directions, sensor_cell, sensor_step):
    count_dir, sx, sy, layers = directions.shape
    depth = count_dir // HALVES
    sensors = sensor_cell.shape[-1]
    assert sensors <= layers // 2 and min(sx, sy) >= 2 * REACH and depth % 16 == 0
    ex_n, ey_n = sx + 2 * REACH, pl.cdiv(sy + 2 * REACH, TILE) * TILE
    vmem = pltpu.VMEM
    wide = sy + 2 * REACH
    both = vmem((HALVES, ex_n, wide, depth, layers), jnp.float32)
    one = vmem((ex_n, wide, depth, layers), jnp.float32)

    def table(n):
        return vmem((n, ex_n, ey_n, layers), jnp.float32)

    tiles = 1 + sum(WIDTHS)
    sems = pltpu.SemaphoreType.DMA
    result = pl.pallas_call(
        functools.partial(kernel, sx, sy, depth),
        out_shape=jax.ShapeDtypeStruct((count_dir, sx * sy, layers), jnp.float32),
        in_specs=[pl.BlockSpec(memory_space=pl.ANY if i == 4 else vmem) for i in range(7)],
        out_specs=pl.BlockSpec(memory_space=pl.ANY),
        scratch_shapes=[
            vmem((count_dir * sx * sy, layers), jnp.float32),
            vmem((HALVES, sx * sy, depth, layers), jnp.float32),
            vmem((STEPS - 1, ex_n, wide, depth, layers), jnp.bfloat16),
            vmem((HALVES, sx + 2, sy + 2, depth, layers), jnp.float32),
            *[both] * 4,
            *[one] * 8,
            table(7),
            table(15),
            table(STEPS - 1),
            vmem((sx, ey_n, layers), jnp.float32),
            vmem((TILE, layers), jnp.int32),
            vmem((PAIRS, 2 * layers, layers), jnp.bfloat16),
            vmem((PAIRS, layers, 2 * layers), jnp.bfloat16),
            vmem((HALVES, PAIRS, depth, layers), jnp.float32),
            vmem((HALVES, PAIRS, depth, layers), jnp.float32),
            vmem((PAIRS, 2, depth, layers), jnp.bfloat16),
            vmem((8, tiles, TILE, layers), jnp.float32),
            vmem((8, tiles, TILE, layers), jnp.float32),
            vmem((8, 2, TILE, layers), jnp.float32),
            vmem((8, 2, TILE, layers), jnp.float32),
            vmem((HALVES, 4, 3, depth, layers), jnp.float32),
            vmem((HALVES, 4, 3, depth, layers), jnp.float32),
            sems(()), sems((HALVES,)),
            sems((8,)), sems((8,)),
            sems((8,)), sems((8,)),
            sems((HALVES, 4)), sems((HALVES, 4)),
            sems((HALVES, 4)), sems((HALVES, 4)),
        ],
        compiler_params=pltpu.CompilerParams(
            collective_id=0, has_side_effects=True, vmem_limit_bytes=56 * 2**20
        ),
    )(
        conc_start, diffusion, courant, uptake,
        directions.reshape(count_dir * sx * sy, layers),
        sensor_cell.reshape(1, sensors), sensor_step.reshape(1, sensors),
    )
    return result.reshape(count_dir, sx, sy, layers)


def solution(mesh):
    in_specs = (
        P("gx", "gy", None),
        P("gx", "gy", None),
        P("gx", "gy", None),
        P("gx", "gy", None),
        P(None, "gx", "gy", None),
        P("gx", "gy", None),
        P("gx", "gy", None),
    )
    out_specs = P(None, "gx", "gy", None)
    return jax.shard_map(
        on_device, mesh=mesh, in_specs=in_specs, out_specs=out_specs, check_vma=False
    )
```

```python
import functools

import jax
import jax.numpy as jnp
from jax import lax
from jax.experimental import pallas as pl
from jax.experimental.pallas import tpu as pltpu
from jax.sharding import PartitionSpec as P

STEPS = 4
REACH = STEPS - 1
HALF_SATURATION = 0.5
PRIOR_WEIGHT = 0.2
PRIOR_SHIFT = 0.5
HALVES = 2
TILE = 8

MESH = pl.DeviceIdType.MESH

NEIGHBOURS = ((-1, 0), (1, 0), (0, -1), (0, 1), (-1, -1), (1, 1), (-1, 1), (1, -1))
OWN = (0, 0)
BLOCKS = (*NEIGHBOURS, OWN)
PAIRS = 5

A1, A2, A3, DZ, BU, DL, DC, R0, R1, R2, R3, N1, N2, N3, N4 = range(15)
C0, DD, UU, WW, C1, C2, C3 = range(7)


WIDTHS = (3, 3, 2, 2)
CORNERS = ((1, 1), (1, 2), (2, 1))


def place_of(block):
    k = BLOCKS.index(block)
    return (k // 2, k % 2)


def corner_cells(f):
    base = sum(w * (w - 1) // 2 for w in WIDTHS[:f])
    return [(i, j, base + r) for r, (i, j) in enumerate(CORNERS[:WIDTHS[f] * (WIDTHS[f] - 1) // 2])]


def shared(d):
    return [b for b in BLOCKS if abs(b[0] - d[0]) <= 1 and abs(b[1] - d[1]) <= 1]


def kernel(
    sx, sy, depth,
    conc_in, diffusion_in, courant_in, uptake_in, dirs_in, cells_in, when_in, out,
    conc, diffusion, courant, uptake, dirs, cells, when, result, marked,
    vp, t1, t2, t3, t4, a4, a3, a2, q4, q3, q2, pl3, pl2,
    ext, coefs, marks, ones, ii, zr, zi, acc, part, ysplit,
    s0, r0, s3, r3, s1, r1,
    in_sem, out_sem,
    s0_send, s0_recv, s3_send, s3_recv, v_send, v_recv, s1_send, s1_recv,
):
    layers = conc.shape[-1]
    fetches = [
        pltpu.make_async_copy(source, target, in_sem.at[i])
        for i, (source, target) in enumerate((
            (conc_in, conc), (diffusion_in, diffusion), (courant_in, courant), (uptake_in, uptake),
            (cells_in, cells), (when_in, when), (dirs_in, dirs),
        ))
    ]
    for fetch in fetches:
        fetch.start()
    half_lanes = layers // 2
    cols = sx * sy
    ex_n, ey_n = ext.shape[1], ext.shape[2]
    lo_x, hi_x, lo_y, hi_y = REACH, REACH + sx, REACH, REACH + sy
    ix, iy = lax.axis_index("gx"), lax.axis_index("gy")
    nx, ny = lax.axis_size("gx"), lax.axis_size("gy")
    have, partner = [], []
    for dx, dy in NEIGHBOURS:
        here = []
        if dx:
            here.append(ix > 0 if dx < 0 else ix < nx - 1)
        if dy:
            here.append(iy > 0 if dy < 0 else iy < ny - 1)
        have.append(functools.reduce(jnp.logical_and, here))
        px = jnp.maximum(ix - 1, 0) if dx < 0 else jnp.minimum(ix + 1, nx - 1) if dx > 0 else ix
        py = jnp.maximum(iy - 1, 0) if dy < 0 else jnp.minimum(iy + 1, ny - 1) if dy > 0 else iy
        partner.append((px, py))
    sides = range(4)
    every = range(8)

    def on(action, ks):
        for k in ks:
            @pl.when(have[k])
            def _(k=k):
                action(k)

    barrier = pltpu.get_barrier_semaphore()
    on(lambda k: pl.semaphore_signal(barrier, inc=1, device_id=partner[k], device_id_type=MESH), every)

    def remote(src, dst, send, recv, k):
        return pltpu.make_async_remote_copy(
            src_ref=src, dst_ref=dst, send_sem=send, recv_sem=recv, device_id=partner[k], device_id_type=MESH
        )

    def size0(k):
        return 1 + sum(WIDTHS) if k < 4 else 2

    def copy0(k):
        n = pl.ds(0, size0(k))
        return remote(s0.at[k, n], r0.at[k ^ 1, n], s0_send.at[k], s0_recv.at[k ^ 1], k)

    def landed0(k):
        n = pl.ds(0, size0(k))
        return remote(r0.at[k, n], r0.at[k, n], s0_send.at[k], s0_recv.at[k], k)

    def size3(k):
        return 2 if k < 4 else 1

    def copy3(k):
        n = pl.ds(0, size3(k))
        return remote(s3.at[k, n], r3.at[k ^ 1, n], s3_send.at[k], s3_recv.at[k ^ 1], k)

    def landed3(k):
        n = pl.ds(0, size3(k))
        return remote(r3.at[k, n], r3.at[k, n], s3_send.at[k], s3_recv.at[k], k)

    def v_at(h, k, halo):
        if k == 0:
            return vp.at[h, 0 if halo else 1, pl.ds(1, sy)]
        if k == 1:
            return vp.at[h, sx + 1 if halo else sx, pl.ds(1, sy)]
        if k == 2:
            return vp.at[h, pl.ds(1, sx), 0 if halo else 1]
        return vp.at[h, pl.ds(1, sx), sy + 1 if halo else sy]

    def copy_v(h, k):
        return remote(v_at(h, k, False), v_at(h, k ^ 1, True), v_send.at[h, k], v_recv.at[h, k ^ 1], k)

    def landed_v(h, k):
        return remote(v_at(h, k, True), v_at(h, k, True), v_send.at[h, k], v_recv.at[h, k], k)

    def size1(k):
        return (len(shared(NEIGHBOURS[k])) + 1) // 2

    def copy1(h, k):
        n = pl.ds(0, size1(k))
        return remote(s1.at[h, k, n], r1.at[h, k ^ 1, n], s1_send.at[h, k], s1_recv.at[h, k ^ 1], k)

    def landed1(h, k):
        n = pl.ds(0, size1(k))
        return remote(r1.at[h, k, n], r1.at[h, k, n], s1_send.at[h, k], s1_recv.at[h, k], k)

    for fetch in fetches[:-1]:
        fetch.wait()
    fields = (conc, diffusion, courant, uptake)
    sensors = cells.shape[1]
    ii[...] = jnp.full(ii.shape, -1, jnp.int32)
    ii[0:1, 0:sensors] = cells[...] // layers + cols * when[...]
    ii[1:2, 0:sensors] = cells[...] % layers
    lane8 = lax.broadcasted_iota(jnp.int32, ii.shape, 1)
    packed = ii[...]
    about = jnp.where(lane8 < half_lanes, packed, pltpu.roll(packed, half_lanes, 1)).astype(jnp.float32)
    for k in every:
        s0[k, 0] = about
    for f, field in enumerate(fields):
        block = field[...]
        base, width = 1 + sum(WIDTHS[:f]), WIDTHS[f]
        for i in range(width):
            s0[0, base + i] = block[i]
            s0[1, base + i] = block[sx - width + i]
            for k, y in ((2, i), (3, sy - width + i)):
                s0[k, base + i] = jnp.concatenate([block[x, y:y + 1] for x in range(sx)], axis=0)
        for k in range(4, 8):
            dx, dy = NEIGHBOURS[k]
            for i, j, r in corner_cells(f):
                x, y = (i - 1 if dx < 0 else sx - i), (j - 1 if dy < 0 else sy - j)
                s0[k, 1, r:r + 1] = block[x, y:y + 1]

    pl.semaphore_wait(barrier, sum(jnp.where(here, 1, 0) for here in have))
    on(lambda k: copy0(k).start(), every)

    fetches[-1].wait()
    for h in range(HALVES):
        @pl.loop(0, sx)
        def _(x, h=h):
            for y in range(sy):
                vp[h, x + 1, y + 1] = dirs[pl.ds(h * depth * cols + x * sy + y, depth, stride=cols), :]

    for k in every:
        @pl.when(jnp.logical_not(have[k]))
        def _(k=k):
            r0[k] = jnp.zeros(r0.shape[1:], jnp.float32)
            r3[k] = jnp.zeros(r3.shape[1:], jnp.float32)
            for h in range(HALVES):
                if k < 4:
                    r1[h, k] = jnp.zeros(r1.shape[2:], jnp.float32)
                    ref = v_at(h, k, True)
                    ref[...] = jnp.zeros(ref.shape, jnp.float32)

    blank = jnp.zeros((depth, layers), jnp.float32)
    for h in range(HALVES):
        for X in (lo_x - 1, hi_x):
            for Y in range(lo_y, hi_y):
                t1[h, X, Y] = blank
            for Y in (lo_y - 1, hi_y):
                t2[h, X, Y] = blank
            for Y in (lo_y - 2, hi_y + 1):
                t3[h, X, Y] = blank
    for X in range(lo_x, hi_x):
        for Y in range(lo_y, hi_y):
            pl3[X, Y] = blank
            pl2[X, Y] = blank
    for f in range(4):
        ext[f] = jnp.zeros(ext.shape[1:], jnp.float32)
    for k in (A1, A2, A3):
        coefs[k] = jnp.zeros(coefs.shape[1:], jnp.float32)
    for f, field in enumerate(fields):
        for x in range(sx):
            ext[f, lo_x + x, pl.ds(lo_y, sy), :] = field[x]

    for X in range(lo_x, hi_x):
        c = ext[C0, X]
        coefs[R0, X] = c / (HALF_SATURATION + c)

    def coef(k, X, Y):
        return coefs[k, X, pl.ds(Y, 1), :]

    def dcoef(X, Y):
        return ext[DD, X, pl.ds(Y, 1), :]

    for h in range(HALVES):
        @pl.loop(lo_x, hi_x)
        def _(X, h=h):
            for Y in range(lo_y, hi_y):
                t1[h, X, Y] = -(vp[h, X - lo_x + 1, Y - lo_y + 1] * coef(R0, X, Y))

    on(lambda k: landed0(k).wait_recv(), every)

    for f in range(4):
        base, width = 1 + sum(WIDTHS[:f]), WIDTHS[f]
        for i in range(width):
            ext[f, lo_x - width + i, pl.ds(lo_y, sy), :] = r0[0, base + i]
            ext[f, hi_x + i, pl.ds(lo_y, sy), :] = r0[1, base + i]
            for k, Y in ((2, lo_y - width + i), (3, hi_y + i)):
                strip = r0[k, base + i]
                for x in range(sx):
                    ext[f, lo_x + x, Y:Y + 1, :] = strip[x:x + 1]
        for k in range(4, 8):
            dx, dy = NEIGHBOURS[k]
            for i, j, r in corner_cells(f):
                X, Y = (lo_x - i if dx < 0 else hi_x + i - 1), (lo_y - j if dy < 0 else hi_y + j - 1)
                ext[f, X, Y:Y + 1, :] = r0[k, 1, r:r + 1]

    layer = lax.broadcasted_iota(jnp.int32, (ey_n, layers), 1)
    first, last = layer == 0, layer == layers - 1

    def lift(f):
        return jnp.where(first, 0.0, pltpu.roll(f, 1, 1))

    def drop(f):
        return jnp.where(last, 0.0, pltpu.roll(f, layers - 1, 1))

    def next_conc(now, later, margin, tail=None):
        for X in range(margin, ex_n - margin):
            c, d, u, w = ext[now, X], ext[DD, X], ext[UU, X], ext[WW, X]
            beside = (
                ext[now, X - 1] + ext[now, X + 1] + pltpu.roll(c, 1, 0) + pltpu.roll(c, ey_n - 1, 0)
                + lift(c) + drop(c)
            )
            carried = u * c
            new = c + d * (beside - 6.0 * c) + lift(carried) - carried - w * c / (HALF_SATURATION + c)
            ext[later, X] = new
            held = HALF_SATURATION + new
            coefs[R1 + later - C1, X] = new / held
            coefs[A1 + later - C1, X] = 1.0 - 6.0 * d - u - w * HALF_SATURATION / (held * held)

    next_conc(C0, C1, 1)
    next_conc(C1, C2, 2)
    next_conc(C2, C3, 3)

    for i in range(2):
        s3[0, i] = coefs[A3, lo_x + i, pl.ds(lo_y, sy), :]
        s3[1, i] = coefs[A3, hi_x - 2 + i, pl.ds(lo_y, sy), :]
        for k, Y in ((2, lo_y + i), (3, hi_y - 2 + i)):
            for x in range(sx):
                s3[k, i, x:x + 1] = coefs[A3, lo_x + x, Y:Y + 1, :]
    for k in range(4, 8):
        dx, dy = NEIGHBOURS[k]
        X, Y = (lo_x if dx < 0 else hi_x - 1), (lo_y if dy < 0 else hi_y - 1)
        s3[k, 0] = jnp.broadcast_to(coefs[A3, X, Y:Y + 1, :], (TILE, layers))
    on(lambda k: copy3(k).start(), every)
    for h in range(HALVES):
        on(lambda k: copy_v(h, k).start(), sides)

    for X in range(1, ex_n - 1):
        d, u = ext[DD, X], ext[UU, X]
        coefs[DZ, X] = jnp.where(last, 0.0, d)
        coefs[BU, X] = jnp.where(first, 0.0, d) + lift(u)
        coefs[DL, X] = lift(d)
        coefs[DC, X] = drop(d) + jnp.where(last, 0.0, u)

    lane1 = lax.broadcasted_iota(jnp.int32, (1, layers), 1)
    keys, depths = {}, {}
    for k, b in enumerate(BLOCKS):
        tile = r0[k, 0] if k < 8 else s0[0, 0]
        low = place_of(b)[1] == 0
        keys[b] = jnp.where((lane1 < half_lanes) == low, tile[0:1], -1.0)
        depths[b] = tile[1:2]
    level = lax.broadcasted_iota(jnp.int32, (layers, layers), 0).astype(jnp.float32)
    for p in range(PAIRS):
        pair = BLOCKS[2 * p:2 * p + 2]
        where = jnp.where(lane1 < half_lanes, depths[pair[0]], depths[pair[-1]])
        hot = jnp.where(level == where, 1.0, 0.0).astype(jnp.bfloat16)
        zr[p, 0:layers] = hot
        zr[p, layers:2 * layers] = hot
        zi[p, :, 0:layers] = hot
        zi[p, :, layers:2 * layers] = hot
    yrow = lax.broadcasted_iota(jnp.int32, (ey_n, layers), 0)
    ymod = (yrow + (sy - REACH % sy)) % sy
    key_at = {
        dx: jnp.where(yrow < lo_y, keys[(dx, -1)], jnp.where(yrow < hi_y, keys[(dx, 0)], keys[(dx, 1)]))
        for dx in (-1, 0, 1)
    }
    for X in range(ex_n):
        dx = -1 if X < lo_x else 1 if X >= hi_x else 0
        name = (((X - REACH) % sx) * sy + ymod).astype(jnp.float32)
        for t in range(1, STEPS + 1):
            mark = jnp.where(key_at[dx] == name + float(cols * t), 1.0, 0.0)
            if t > 1:
                marks[t - 2, X] = mark
            elif dx == 0:
                ones[X - lo_x] = mark
    for t in range(1, STEPS + 1):
        mark = ones[...] if t == 1 else marks[t - 2, pl.ds(lo_x, sx)]
        count = lax.dot_general(
            mark.reshape(sx * ey_n, layers).astype(jnp.bfloat16), zi[PAIRS - 1, :, 0:layers],
            (((1,), (1,)), ((), ())), preferred_element_type=jnp.float32,
        )
        coefs[N1 + t - 1, pl.ds(lo_x, sx)] = count.reshape(sx, ey_n, layers)

    def up(f):
        return pltpu.roll(f, 1, 1)

    def down(f):
        return pltpu.roll(f, layers - 1, 1)

    def add(terms):
        return functools.reduce(lambda p, q: p + q, terms)

    def rows(reach, body):
        for X in range(lo_x, hi_x):
            body(X, 0, 0)
        for j in range(1, reach + 1):
            body(lo_x - j, j, 1)
            body(hi_x + j - 1, j, -1)

    def out_y(Y):
        return max(0, lo_y - Y, Y - hi_y + 1)

    def tangent_row(h, reach, prev, new, ka, kr, X, ex, inward):
        held = reach - 1
        mid = {}
        if ex <= held:
            mid = {Y: prev[h, X, Y] for Y in range(lo_y - held + ex, hi_y + held - ex)}
        for Y in range(lo_y - reach + ex, hi_y + reach - ex):
            ey = out_y(Y)
            terms = [mid[near] for near in (Y - 1, Y + 1) if near in mid]
            if ex == 0:
                if ey <= held:
                    terms += [prev[h, X - 1, Y], prev[h, X + 1, Y]]
            else:
                terms.append(prev[h, X + inward, Y])
                if ex + 1 + ey <= held:
                    terms.append(prev[h, X - inward, Y])
            value = dcoef(X, Y) * add(terms)
            if ex + ey < reach:
                p = mid[Y]
                value = (
                    value + coef(ka, X, Y) * p + coef(DZ, X, Y) * down(p) + coef(BU, X, Y) * up(p)
                )
                if ex == 0 and ey == 0:
                    value = value - coef(kr, X, Y) * vp[h, X - lo_x + 1, Y - lo_y + 1]
            new[h, X, Y] = value

    def block_of(X, Y):
        return (
            -1 if X < lo_x else 1 if X >= hi_x else 0,
            -1 if Y < lo_y else 1 if Y >= hi_y else 0,
        )

    def touched(p, reach):
        found = []
        for X in range(ex_n):
            for Y in range(lo_y + sy + REACH):
                b = block_of(X, Y)
                if place_of(b)[0] != p:
                    continue
                if b == OWN:
                    near = min(X - lo_x, hi_x - 1 - X, Y - lo_y, hi_y - 1 - Y) < reach
                else:
                    near = max(0, lo_x - X, X - hi_x + 1) + out_y(Y) <= reach
                if near:
                    found.append((X, Y))
        return found

    chunk = 16

    def read(h, p, wanted):
        total = None
        for start in range(0, len(wanted), chunk):
            some = wanted[start:start + chunk]
            high, low = [], []
            for field, t, X, Y in some:
                value = field[h, X, Y]
                top = value.astype(jnp.bfloat16)
                high.append(top)
                low.append((value - top.astype(jnp.float32)).astype(jnp.bfloat16))
            left = jnp.concatenate([jnp.concatenate(high, axis=0), jnp.concatenate(low, axis=0)], axis=1)
            got = lax.dot_general(left, zr[p], (((1,), (0,)), ((), ())), preferred_element_type=jnp.float32)
            for i, (field, t, X, Y) in enumerate(some):
                term = got[i * depth:(i + 1) * depth] * marks[t - 2, X, pl.ds(Y, 1), :]
                total = term if total is None else total + term
        return total

    @pl.loop(0, HALVES)
    def _(h):
        rows(1, functools.partial(tangent_row, h, 1, t1, t2, A1, R1))
        rows(2, functools.partial(tangent_row, h, 2, t2, t3, A2, R2))
        for p in range(PAIRS):
            acc[h, p] = read(
                h, p, [(t2, 2, *at) for at in touched(p, 1)] + [(t3, 3, *at) for at in touched(p, 2)]
            )

    on(lambda k: landed3(k).wait_recv(), every)
    for i in range(2):
        coefs[A3, lo_x - 2 + i, pl.ds(lo_y, sy), :] = r3[0, i]
        coefs[A3, hi_x + i, pl.ds(lo_y, sy), :] = r3[1, i]
        for k, Y in ((2, lo_y - 2 + i), (3, hi_y + i)):
            for x in range(sx):
                coefs[A3, lo_x + x, Y:Y + 1, :] = r3[k, i, x:x + 1]
    for k in range(4, 8):
        dx, dy = NEIGHBOURS[k]
        X, Y = (lo_x - 1 if dx < 0 else hi_x), (lo_y - 1 if dy < 0 else hi_y)
        coefs[A3, X, Y:Y + 1, :] = r3[k, 0, 0:1]

    lane = lax.broadcasted_iota(jnp.int32, (depth, layers), 1)
    lower = lane < half_lanes

    def moved(value, source, target):
        return value if source == target else pltpu.roll(value, half_lanes, 1)

    def send_sums(h, sums, ks):
        for k in ks:
            need = shared(NEIGHBOURS[k])
            for j in range(0, len(need), 2):
                (pa, ha), (pb, hb) = place_of(need[j]), place_of(need[j + 1])
                s1[h, k, j // 2] = jnp.where(lower, moved(sums[pa], ha, 0), moved(sums[pb], hb, 1))
        on(lambda k: copy1(h, k).start(), ks)

    def add_sums(h, sums, ks):
        on(lambda k: landed1(h, k).wait_recv(), ks)
        for k in ks:
            d, need = NEIGHBOURS[k], shared(NEIGHBOURS[k ^ 1])
            for j, b in enumerate(need):
                p, target = place_of((b[0] + d[0], b[1] + d[1]))
                value = moved(r1[h, k, j // 2], j % 2, target)
                sums[p] = sums[p] + jnp.where(lower == (target == 0), value, 0.0)
        return sums

    def relay(h):
        sums = add_sums(h, [part[h, p] for p in range(PAIRS - 1)] + [blank], (2, 3))
        own = part[h, PAIRS - 1]
        for p in range(PAIRS):
            part[h, p] = sums[p]
        send_sums(h, sums[:-1] + [sums[-1] + own], (0, 1))

    @pl.loop(0, HALVES)
    def _(h):
        rows(3, functools.partial(tangent_row, h, 3, t3, t4, A3, R3))
        mine = []
        for p in range(PAIRS):
            mine.append(acc[h, p] + read(h, p, [(t4, 4, *at) for at in touched(p, 3)]))
            part[h, p] = mine[p]
        send_sums(h, mine, (2, 3))

    not_first = jnp.where(lane1 == 0, 0.0, 1.0)
    not_last = jnp.where(lane1 == layers - 1, 0.0, 1.0)

    def prior(h):
        for x in range(sx):
            X = x + lo_x
            mid = [vp[h, x + 1, y + 1] for y in range(sy)]
            for y in range(sy):
                Y = y + lo_y
                v = mid[y]
                near = [vp[h, i + 1, y + 1] for i in (x - 1, x + 1) if 0 <= i < sx]
                near += [mid[j] for j in (y - 1, y + 1) if 0 <= j < sy]
                beside = add(near) + not_first * up(v) + not_last * down(v)
                first_sensors = coef(R0, X, Y) * (coef(N1, X, Y) * t1[h, X, Y])
                result[h, x * sy + y] = (
                    PRIOR_WEIGHT * ((6.0 + PRIOR_SHIFT) * v - beside) - first_sensors
                )

    for h in range(HALVES):
        prior(h)
        relay(h)

    for p in range(PAIRS):
        for t in range(2, STEPS + 1):
            for X, Y in touched(p, t - 1):
                mark = jnp.broadcast_to(marks[t - 2, X, pl.ds(Y, 1), :], (depth, layers))
                marked[t - 2, X, Y] = mark.astype(jnp.bfloat16)

    def inject(p, t, reach, use):
        wanted = touched(p, reach)
        for start in range(0, len(wanted), chunk):
            some = wanted[start:start + chunk]
            high, low = [], []
            for X, Y in some:
                mark = marked[t - 2, X, Y]
                high.append(ysplit[p, 0] * mark)
                low.append(ysplit[p, 1] * mark)
            left = jnp.concatenate([jnp.concatenate(high, axis=0), jnp.concatenate(low, axis=0)], axis=1)
            got = lax.dot_general(left, zi[p], (((1,), (1,)), ((), ())), preferred_element_type=jnp.float32)
            for i, (X, Y) in enumerate(some):
                use(X, Y, got[i * depth:(i + 1) * depth])

    def adjoint(hold, q, ka, X, Y, centre):
        a = hold[X, Y] if centre is None else centre
        return (
            coef(ka, X, Y) * a
            + ((q[X - 1, Y] + q[X + 1, Y]) + (q[X, Y - 1] + q[X, Y + 1]))
            + coef(DL, X, Y) * up(a)
            + coef(DC, X, Y) * down(a)
        )

    def adjoint_row(h, reach, hold, q, new_hold, new_q, placed, tangent, ka, kn, X, ex, inward):
        for Y in range(lo_y - reach + ex, hi_y + reach - ex):
            a = adjoint(hold, q, ka, X, Y, None) + placed[X, Y]
            if ex == 0 and out_y(Y) == 0:
                a = a + coef(kn, X, Y) * tangent[h, X, Y]
            new_hold[X, Y] = a
            new_q[X, Y] = dcoef(X, Y) * a

    inner = [
        (X, Y) for X in range(lo_x, hi_x) for Y in range(lo_y, hi_y) if (X, Y) not in touched(PAIRS - 1, 3)
    ]

    @pl.loop(0, HALVES)
    def _(h):
        total = add_sums(h, [part[h, p] for p in range(PAIRS)], (0, 1))
        for p in range(PAIRS):
            top = total[p].astype(jnp.bfloat16)
            ysplit[p, 0] = top
            ysplit[p, 1] = (total[p] - top.astype(jnp.float32)).astype(jnp.bfloat16)

        def last_step(X, Y, value):
            a4[X, Y] = value
            q4[X, Y] = dcoef(X, Y) * value

        def last_own(X, Y, value):
            last_step(X, Y, value + coef(N4, X, Y) * t4[h, X, Y])

        def to_three(X, Y, value):
            pl3[X, Y] = value

        def to_two(X, Y, value):
            pl2[X, Y] = value

        for p in range(PAIRS):
            inject(p, 4, 3, last_own if p == PAIRS - 1 else last_step)
            inject(p, 3, 2, to_three)
            inject(p, 2, 1, to_two)
        for X, Y in inner:
            last_step(X, Y, coef(N4, X, Y) * t4[h, X, Y])
        rows(2, functools.partial(adjoint_row, h, 2, a4, q4, a3, q3, pl3, t3, A3, N3))
        rows(1, functools.partial(adjoint_row, h, 1, a3, q3, a2, q2, pl2, t2, A2, N2))
        on(lambda k: landed_v(h, k).wait_recv(), sides)

        for x in range(sx):
            X = x + lo_x
            for y in range(sy):
                Y = y + lo_y
                middle = a2[X, Y]
                gradient = (
                    coef(R3, X, Y) * a4[X, Y] + coef(R2, X, Y) * a3[X, Y] + coef(R1, X, Y) * middle
                    + coef(R0, X, Y) * adjoint(a2, q2, A1, X, Y, middle)
                )
                outside = [vp[h, i, y + 1] for i in (0, sx + 1) if abs(i - x - 1) == 1]
                outside += [vp[h, x + 1, j] for j in (0, sy + 1) if abs(j - y - 1) == 1]
                if outside:
                    gradient = gradient + PRIOR_WEIGHT * add(outside)
                at = x * sy + y
                result[h, at] = result[h, at] - gradient
                pltpu.make_async_copy(
                    result.at[h, at], out.at[pl.ds(h * depth, depth), at], out_sem.at[h]
                ).start()

    for h in range(HALVES):
        pltpu.make_async_copy(result.at[h], result.at[h], out_sem.at[h]).wait()
    on(lambda k: copy0(k).wait_send(), every)
    on(lambda k: copy3(k).wait_send(), every)
    for h in range(HALVES):
        on(lambda k: copy_v(h, k).wait_send(), sides)
        on(lambda k: copy1(h, k).wait_send(), sides)


def on_device(conc_start, diffusion, courant, uptake, directions, sensor_cell, sensor_step):
    count_dir, sx, sy, layers = directions.shape
    depth = count_dir // HALVES
    sensors = sensor_cell.shape[-1]
    assert sensors <= layers // 2 and min(sx, sy) >= 2 * REACH and depth % 16 == 0
    ex_n, ey_n = sx + 2 * REACH, pl.cdiv(sy + 2 * REACH, TILE) * TILE
    vmem = pltpu.VMEM
    wide = sy + 2 * REACH
    both = vmem((HALVES, ex_n, wide, depth, layers), jnp.float32)
    one = vmem((ex_n, wide, depth, layers), jnp.float32)

    def table(n):
        return vmem((n, ex_n, ey_n, layers), jnp.float32)

    tiles = 1 + sum(WIDTHS)
    sems = pltpu.SemaphoreType.DMA
    result = pl.pallas_call(
        functools.partial(kernel, sx, sy, depth),
        out_shape=jax.ShapeDtypeStruct((count_dir, sx * sy, layers), jnp.float32),
        in_specs=[pl.BlockSpec(memory_space=pltpu.HBM)] * 7,
        out_specs=pl.BlockSpec(memory_space=pl.ANY),
        scratch_shapes=[
            *[vmem((sx, sy, layers), jnp.float32)] * 4,
            vmem((count_dir * sx * sy, layers), jnp.float32),
            *[vmem((1, sensors), jnp.int32)] * 2,
            vmem((HALVES, sx * sy, depth, layers), jnp.float32),
            vmem((STEPS - 1, ex_n, wide, depth, layers), jnp.bfloat16),
            vmem((HALVES, sx + 2, sy + 2, depth, layers), jnp.float32),
            *[both] * 4,
            *[one] * 8,
            table(7),
            table(15),
            table(STEPS - 1),
            vmem((sx, ey_n, layers), jnp.float32),
            vmem((TILE, layers), jnp.int32),
            vmem((PAIRS, 2 * layers, layers), jnp.bfloat16),
            vmem((PAIRS, layers, 2 * layers), jnp.bfloat16),
            vmem((HALVES, PAIRS, depth, layers), jnp.float32),
            vmem((HALVES, PAIRS, depth, layers), jnp.float32),
            vmem((PAIRS, 2, depth, layers), jnp.bfloat16),
            vmem((8, tiles, TILE, layers), jnp.float32),
            vmem((8, tiles, TILE, layers), jnp.float32),
            vmem((8, 2, TILE, layers), jnp.float32),
            vmem((8, 2, TILE, layers), jnp.float32),
            vmem((HALVES, 4, 3, depth, layers), jnp.float32),
            vmem((HALVES, 4, 3, depth, layers), jnp.float32),
            sems((7,)), sems((HALVES,)),
            sems((8,)), sems((8,)),
            sems((8,)), sems((8,)),
            sems((HALVES, 4)), sems((HALVES, 4)),
            sems((HALVES, 4)), sems((HALVES, 4)),
        ],
        compiler_params=pltpu.CompilerParams(
            collective_id=0, has_side_effects=True, vmem_limit_bytes=56 * 2**20
        ),
    )(
        conc_start, diffusion, courant, uptake,
        directions.reshape(count_dir * sx * sy, layers),
        sensor_cell.reshape(1, sensors), sensor_step.reshape(1, sensors),
    )
    return result.reshape(count_dir, sx, sy, layers)


def solution(mesh):
    in_specs = (
        P("gx", "gy", None),
        P("gx", "gy", None),
        P("gx", "gy", None),
        P("gx", "gy", None),
        P(None, "gx", "gy", None),
        P("gx", "gy", None),
        P("gx", "gy", None),
    )
    out_specs = P(None, "gx", "gy", None)
    return jax.shard_map(
        on_device, mesh=mesh, in_specs=in_specs, out_specs=out_specs, check_vma=False
    )
```

```python
import functools

import jax
import jax.numpy as jnp
from jax import lax
from jax.experimental import pallas as pl
from jax.experimental.pallas import tpu as pltpu
from jax.sharding import PartitionSpec as P

STEPS = 4
REACH = STEPS - 1
HALF_SATURATION = 0.5
PRIOR_WEIGHT = 0.2
PRIOR_SHIFT = 0.5
HALVES = 2
TILE = 8

MESH = pl.DeviceIdType.MESH

NEIGHBOURS = ((-1, 0), (1, 0), (0, -1), (0, 1), (-1, -1), (1, 1), (-1, 1), (1, -1))
OWN = (0, 0)
BLOCKS = (*NEIGHBOURS, OWN)
PAIRS = 5

A1, A2, A3, DZ, BU, DL, DC, R0, R1, R2, R3, N1, N2, N3, N4 = range(15)
C0, DD, UU, WW, C1, C2, C3 = range(7)


WIDTHS = (3, 3, 2, 2)
CORNERS = ((1, 1), (1, 2), (2, 1))


def place_of(block):
    k = BLOCKS.index(block)
    return (k // 2, k % 2)


def corner_cells(f):
    base = sum(w * (w - 1) // 2 for w in WIDTHS[:f])
    return [(i, j, base + r) for r, (i, j) in enumerate(CORNERS[:WIDTHS[f] * (WIDTHS[f] - 1) // 2])]


def shared(d):
    return [b for b in BLOCKS if abs(b[0] - d[0]) <= 1 and abs(b[1] - d[1]) <= 1]


def kernel(
    sx, sy, depth,
    conc_in, diffusion_in, courant_in, uptake_in, dirs_in, cells_in, when_in, out,
    conc, diffusion, courant, uptake, dirs, cells, when, result, marked,
    vp, t1, t2, t3, t4, a4, a3, a2, q4, q3, q2, pl3, pl2,
    ext, coefs, marks, ones, ii, zr, zi, acc, part, ysplit,
    s0, r0, s3, r3, s1, r1,
    in_sem, out_sem,
    s0_send, s0_recv, s3_send, s3_recv, v_send, v_recv, s1_send, s1_recv,
):
    layers = conc.shape[-1]
    fetches = [
        pltpu.make_async_copy(source, target, in_sem.at[i])
        for i, (source, target) in enumerate((
            (conc_in, conc), (diffusion_in, diffusion), (courant_in, courant), (uptake_in, uptake),
            (cells_in, cells), (when_in, when), (dirs_in, dirs),
        ))
    ]
    for fetch in fetches:
        fetch.start()
    half_lanes = layers // 2
    cols = sx * sy
    ex_n, ey_n = ext.shape[1], ext.shape[2]
    lo_x, hi_x, lo_y, hi_y = REACH, REACH + sx, REACH, REACH + sy
    ix, iy = lax.axis_index("gx"), lax.axis_index("gy")
    nx, ny = lax.axis_size("gx"), lax.axis_size("gy")
    have, partner = [], []
    for dx, dy in NEIGHBOURS:
        here = []
        if dx:
            here.append(ix > 0 if dx < 0 else ix < nx - 1)
        if dy:
            here.append(iy > 0 if dy < 0 else iy < ny - 1)
        have.append(functools.reduce(jnp.logical_and, here))
        px = jnp.maximum(ix - 1, 0) if dx < 0 else jnp.minimum(ix + 1, nx - 1) if dx > 0 else ix
        py = jnp.maximum(iy - 1, 0) if dy < 0 else jnp.minimum(iy + 1, ny - 1) if dy > 0 else iy
        partner.append((px, py))
    sides = range(4)
    every = range(8)

    def on(action, ks):
        for k in ks:
            @pl.when(have[k])
            def _(k=k):
                action(k)

    barrier = pltpu.get_barrier_semaphore()
    on(lambda k: pl.semaphore_signal(barrier, inc=1, device_id=partner[k], device_id_type=MESH), every)

    def remote(src, dst, send, recv, k):
        return pltpu.make_async_remote_copy(
            src_ref=src, dst_ref=dst, send_sem=send, recv_sem=recv, device_id=partner[k], device_id_type=MESH
        )

    def size0(k):
        return 1 + sum(WIDTHS) if k < 4 else 2

    def copy0(k):
        n = pl.ds(0, size0(k))
        return remote(s0.at[k, n], r0.at[k ^ 1, n], s0_send.at[k], s0_recv.at[k ^ 1], k)

    def landed0(k):
        n = pl.ds(0, size0(k))
        return remote(r0.at[k, n], r0.at[k, n], s0_send.at[k], s0_recv.at[k], k)

    def size3(k):
        return 2 if k < 4 else 1

    def copy3(k):
        n = pl.ds(0, size3(k))
        return remote(s3.at[k, n], r3.at[k ^ 1, n], s3_send.at[k], s3_recv.at[k ^ 1], k)

    def landed3(k):
        n = pl.ds(0, size3(k))
        return remote(r3.at[k, n], r3.at[k, n], s3_send.at[k], s3_recv.at[k], k)

    def v_at(h, k, halo):
        if k == 0:
            return vp.at[h, 0 if halo else 1, pl.ds(1, sy)]
        if k == 1:
            return vp.at[h, sx + 1 if halo else sx, pl.ds(1, sy)]
        if k == 2:
            return vp.at[h, pl.ds(1, sx), 0 if halo else 1]
        return vp.at[h, pl.ds(1, sx), sy + 1 if halo else sy]

    def copy_v(h, k):
        return remote(v_at(h, k, False), v_at(h, k ^ 1, True), v_send.at[h, k], v_recv.at[h, k ^ 1], k)

    def landed_v(h, k):
        return remote(v_at(h, k, True), v_at(h, k, True), v_send.at[h, k], v_recv.at[h, k], k)

    def size1(k):
        return (len(shared(NEIGHBOURS[k])) + 1) // 2

    def copy1(h, k):
        n = pl.ds(0, size1(k))
        return remote(s1.at[h, k, n], r1.at[h, k ^ 1, n], s1_send.at[h, k], s1_recv.at[h, k ^ 1], k)

    def landed1(h, k):
        n = pl.ds(0, size1(k))
        return remote(r1.at[h, k, n], r1.at[h, k, n], s1_send.at[h, k], s1_recv.at[h, k], k)

    for fetch in fetches[:-1]:
        fetch.wait()
    fields = (conc, diffusion, courant, uptake)
    sensors = cells.shape[1]
    ii[...] = jnp.full(ii.shape, -1, jnp.int32)
    ii[0:1, 0:sensors] = cells[...] // layers + cols * when[...]
    ii[1:2, 0:sensors] = cells[...] % layers
    lane8 = lax.broadcasted_iota(jnp.int32, ii.shape, 1)
    packed = ii[...]
    about = jnp.where(lane8 < half_lanes, packed, pltpu.roll(packed, half_lanes, 1)).astype(jnp.float32)
    for k in every:
        s0[k, 0] = about
    for f, field in enumerate(fields):
        block = field[...]
        base, width = 1 + sum(WIDTHS[:f]), WIDTHS[f]
        for i in range(width):
            s0[0, base + i] = block[i]
            s0[1, base + i] = block[sx - width + i]
            for k, y in ((2, i), (3, sy - width + i)):
                s0[k, base + i] = jnp.concatenate([block[x, y:y + 1] for x in range(sx)], axis=0)
        for k in range(4, 8):
            dx, dy = NEIGHBOURS[k]
            for i, j, r in corner_cells(f):
                x, y = (i - 1 if dx < 0 else sx - i), (j - 1 if dy < 0 else sy - j)
                s0[k, 1, r:r + 1] = block[x, y:y + 1]

    pl.semaphore_wait(barrier, sum(jnp.where(here, 1, 0) for here in have))
    on(lambda k: copy0(k).start(), every)

    fetches[-1].wait()
    for h in range(HALVES):
        @pl.loop(0, sx)
        def _(x, h=h):
            for y in range(sy):
                vp[h, x + 1, y + 1] = dirs[pl.ds(h * depth * cols + x * sy + y, depth, stride=cols), :]

    for k in every:
        @pl.when(jnp.logical_not(have[k]))
        def _(k=k):
            r0[k] = jnp.zeros(r0.shape[1:], jnp.float32)
            r3[k] = jnp.zeros(r3.shape[1:], jnp.float32)
            for h in range(HALVES):
                if k < 4:
                    r1[h, k] = jnp.zeros(r1.shape[2:], jnp.float32)
                    ref = v_at(h, k, True)
                    ref[...] = jnp.zeros(ref.shape, jnp.float32)

    blank = jnp.zeros((depth, layers), jnp.float32)
    for h in range(HALVES):
        for X in (lo_x - 1, hi_x):
            for Y in range(lo_y, hi_y):
                t1[h, X, Y] = blank
            for Y in (lo_y - 1, hi_y):
                t2[h, X, Y] = blank
            for Y in (lo_y - 2, hi_y + 1):
                t3[h, X, Y] = blank
    for X in range(lo_x, hi_x):
        for Y in range(lo_y, hi_y):
            pl3[X, Y] = blank
            pl2[X, Y] = blank
    for f in range(4):
        ext[f] = jnp.zeros(ext.shape[1:], jnp.float32)
    for k in (A1, A2, A3):
        coefs[k] = jnp.zeros(coefs.shape[1:], jnp.float32)
    for f, field in enumerate(fields):
        for x in range(sx):
            ext[f, lo_x + x, pl.ds(lo_y, sy), :] = field[x]

    for X in range(lo_x, hi_x):
        c = ext[C0, X]
        coefs[R0, X] = c / (HALF_SATURATION + c)

    def coef(k, X, Y):
        return coefs[k, X, pl.ds(Y, 1), :]

    def dcoef(X, Y):
        return ext[DD, X, pl.ds(Y, 1), :]

    for h in range(HALVES):
        @pl.loop(lo_x, hi_x)
        def _(X, h=h):
            for Y in range(lo_y, hi_y):
                t1[h, X, Y] = -(vp[h, X - lo_x + 1, Y - lo_y + 1] * coef(R0, X, Y))

    on(lambda k: landed0(k).wait_recv(), every)

    for f in range(4):
        base, width = 1 + sum(WIDTHS[:f]), WIDTHS[f]
        for i in range(width):
            ext[f, lo_x - width + i, pl.ds(lo_y, sy), :] = r0[0, base + i]
            ext[f, hi_x + i, pl.ds(lo_y, sy), :] = r0[1, base + i]
            for k, Y in ((2, lo_y - width + i), (3, hi_y + i)):
                strip = r0[k, base + i]
                for x in range(sx):
                    ext[f, lo_x + x, Y:Y + 1, :] = strip[x:x + 1]
        for k in range(4, 8):
            dx, dy = NEIGHBOURS[k]
            for i, j, r in corner_cells(f):
                X, Y = (lo_x - i if dx < 0 else hi_x + i - 1), (lo_y - j if dy < 0 else hi_y + j - 1)
                ext[f, X, Y:Y + 1, :] = r0[k, 1, r:r + 1]

    layer = lax.broadcasted_iota(jnp.int32, (ey_n, layers), 1)
    first, last = layer == 0, layer == layers - 1

    def lift(f):
        return jnp.where(first, 0.0, pltpu.roll(f, 1, 1))

    def drop(f):
        return jnp.where(last, 0.0, pltpu.roll(f, layers - 1, 1))

    def next_conc(now, later, margin, tail=None):
        for X in range(margin, ex_n - margin):
            c, d, u, w = ext[now, X], ext[DD, X], ext[UU, X], ext[WW, X]
            beside = (
                ext[now, X - 1] + ext[now, X + 1] + pltpu.roll(c, 1, 0) + pltpu.roll(c, ey_n - 1, 0)
                + lift(c) + drop(c)
            )
            carried = u * c
            new = c + d * (beside - 6.0 * c) + lift(carried) - carried - w * c / (HALF_SATURATION + c)
            ext[later, X] = new
            held = HALF_SATURATION + new
            coefs[R1 + later - C1, X] = new / held
            coefs[A1 + later - C1, X] = 1.0 - 6.0 * d - u - w * HALF_SATURATION / (held * held)

    next_conc(C0, C1, 1)
    next_conc(C1, C2, 2)
    next_conc(C2, C3, 3)

    for i in range(2):
        s3[0, i] = coefs[A3, lo_x + i, pl.ds(lo_y, sy), :]
        s3[1, i] = coefs[A3, hi_x - 2 + i, pl.ds(lo_y, sy), :]
        for k, Y in ((2, lo_y + i), (3, hi_y - 2 + i)):
            for x in range(sx):
                s3[k, i, x:x + 1] = coefs[A3, lo_x + x, Y:Y + 1, :]
    for k in range(4, 8):
        dx, dy = NEIGHBOURS[k]
        X, Y = (lo_x if dx < 0 else hi_x - 1), (lo_y if dy < 0 else hi_y - 1)
        s3[k, 0] = jnp.broadcast_to(coefs[A3, X, Y:Y + 1, :], (TILE, layers))
    on(lambda k: copy3(k).start(), every)
    for h in range(HALVES):
        on(lambda k: copy_v(h, k).start(), sides)

    for X in range(1, ex_n - 1):
        d, u = ext[DD, X], ext[UU, X]
        coefs[DZ, X] = jnp.where(last, 0.0, d)
        coefs[BU, X] = jnp.where(first, 0.0, d) + lift(u)
        coefs[DL, X] = lift(d)
        coefs[DC, X] = drop(d) + jnp.where(last, 0.0, u)

    lane1 = lax.broadcasted_iota(jnp.int32, (1, layers), 1)
    keys, depths = {}, {}
    for k, b in enumerate(BLOCKS):
        tile = r0[k, 0] if k < 8 else s0[0, 0]
        low = place_of(b)[1] == 0
        keys[b] = jnp.where((lane1 < half_lanes) == low, tile[0:1], -1.0)
        depths[b] = tile[1:2]
    level = lax.broadcasted_iota(jnp.int32, (layers, layers), 0).astype(jnp.float32)
    for p in range(PAIRS):
        pair = BLOCKS[2 * p:2 * p + 2]
        where = jnp.where(lane1 < half_lanes, depths[pair[0]], depths[pair[-1]])
        hot = jnp.where(level == where, 1.0, 0.0).astype(jnp.bfloat16)
        zr[p, 0:layers] = hot
        zr[p, layers:2 * layers] = hot
        zi[p, :, 0:layers] = hot
        zi[p, :, layers:2 * layers] = hot
    yrow = lax.broadcasted_iota(jnp.int32, (ey_n, layers), 0)
    ymod = (yrow + (sy - REACH % sy)) % sy
    key_at = {
        dx: jnp.where(yrow < lo_y, keys[(dx, -1)], jnp.where(yrow < hi_y, keys[(dx, 0)], keys[(dx, 1)]))
        for dx in (-1, 0, 1)
    }
    for X in range(ex_n):
        dx = -1 if X < lo_x else 1 if X >= hi_x else 0
        name = (((X - REACH) % sx) * sy + ymod).astype(jnp.float32)
        for t in range(1, STEPS + 1):
            mark = jnp.where(key_at[dx] == name + float(cols * t), 1.0, 0.0)
            if t > 1:
                marks[t - 2, X] = mark
            elif dx == 0:
                ones[X - lo_x] = mark
    for t in range(1, STEPS + 1):
        mark = ones[...] if t == 1 else marks[t - 2, pl.ds(lo_x, sx)]
        count = lax.dot_general(
            mark.reshape(sx * ey_n, layers).astype(jnp.bfloat16), zi[PAIRS - 1, :, 0:layers],
            (((1,), (1,)), ((), ())), preferred_element_type=jnp.float32,
        )
        coefs[N1 + t - 1, pl.ds(lo_x, sx)] = count.reshape(sx, ey_n, layers)

    def up(f):
        return pltpu.roll(f, 1, 1)

    def down(f):
        return pltpu.roll(f, layers - 1, 1)

    def add(terms):
        return functools.reduce(lambda p, q: p + q, terms)

    def rows(reach, body):
        for X in range(lo_x, hi_x):
            body(X, 0, 0)
        for j in range(1, reach + 1):
            body(lo_x - j, j, 1)
            body(hi_x + j - 1, j, -1)

    def out_y(Y):
        return max(0, lo_y - Y, Y - hi_y + 1)

    def tangent_row(h, reach, prev, new, ka, kr, X, ex, inward):
        held = reach - 1
        mid = {}
        if ex <= held:
            mid = {Y: prev[h, X, Y] for Y in range(lo_y - held + ex, hi_y + held - ex)}
        for Y in range(lo_y - reach + ex, hi_y + reach - ex):
            ey = out_y(Y)
            terms = [mid[near] for near in (Y - 1, Y + 1) if near in mid]
            if ex == 0:
                if ey <= held:
                    terms += [prev[h, X - 1, Y], prev[h, X + 1, Y]]
            else:
                terms.append(prev[h, X + inward, Y])
                if ex + 1 + ey <= held:
                    terms.append(prev[h, X - inward, Y])
            value = dcoef(X, Y) * add(terms)
            if ex + ey < reach:
                p = mid[Y]
                value = (
                    value + coef(ka, X, Y) * p + coef(DZ, X, Y) * down(p) + coef(BU, X, Y) * up(p)
                )
                if ex == 0 and ey == 0:
                    value = value - coef(kr, X, Y) * vp[h, X - lo_x + 1, Y - lo_y + 1]
            new[h, X, Y] = value

    def block_of(X, Y):
        return (
            -1 if X < lo_x else 1 if X >= hi_x else 0,
            -1 if Y < lo_y else 1 if Y >= hi_y else 0,
        )

    def touched(p, reach):
        found = []
        for X in range(ex_n):
            for Y in range(lo_y + sy + REACH):
                b = block_of(X, Y)
                if place_of(b)[0] != p:
                    continue
                if b == OWN:
                    near = min(X - lo_x, hi_x - 1 - X, Y - lo_y, hi_y - 1 - Y) < reach
                else:
                    near = max(0, lo_x - X, X - hi_x + 1) + out_y(Y) <= reach
                if near:
                    found.append((X, Y))
        return found

    chunk = 16

    def read(h, p, wanted):
        total = None
        for start in range(0, len(wanted), chunk):
            some = wanted[start:start + chunk]
            high, low = [], []
            for field, t, X, Y in some:
                value = field[h, X, Y]
                top = value.astype(jnp.bfloat16)
                high.append(top)
                low.append((value - top.astype(jnp.float32)).astype(jnp.bfloat16))
            left = jnp.concatenate([jnp.concatenate(high, axis=0), jnp.concatenate(low, axis=0)], axis=1)
            got = lax.dot_general(left, zr[p], (((1,), (0,)), ((), ())), preferred_element_type=jnp.float32)
            for i, (field, t, X, Y) in enumerate(some):
                term = got[i * depth:(i + 1) * depth] * marks[t - 2, X, pl.ds(Y, 1), :]
                total = term if total is None else total + term
        return total

    @pl.loop(0, HALVES)
    def _(h):
        rows(1, functools.partial(tangent_row, h, 1, t1, t2, A1, R1))
        rows(2, functools.partial(tangent_row, h, 2, t2, t3, A2, R2))
        for p in range(PAIRS):
            acc[h, p] = read(
                h, p, [(t2, 2, *at) for at in touched(p, 1)] + [(t3, 3, *at) for at in touched(p, 2)]
            )

    on(lambda k: landed3(k).wait_recv(), every)
    for i in range(2):
        coefs[A3, lo_x - 2 + i, pl.ds(lo_y, sy), :] = r3[0, i]
        coefs[A3, hi_x + i, pl.ds(lo_y, sy), :] = r3[1, i]
        for k, Y in ((2, lo_y - 2 + i), (3, hi_y + i)):
            for x in range(sx):
                coefs[A3, lo_x + x, Y:Y + 1, :] = r3[k, i, x:x + 1]
    for k in range(4, 8):
        dx, dy = NEIGHBOURS[k]
        X, Y = (lo_x - 1 if dx < 0 else hi_x), (lo_y - 1 if dy < 0 else hi_y)
        coefs[A3, X, Y:Y + 1, :] = r3[k, 0, 0:1]

    lane = lax.broadcasted_iota(jnp.int32, (depth, layers), 1)
    lower = lane < half_lanes

    def moved(value, source, target):
        return value if source == target else pltpu.roll(value, half_lanes, 1)

    def send_sums(h, sums, ks):
        for k in ks:
            need = shared(NEIGHBOURS[k])
            for j in range(0, len(need), 2):
                (pa, ha), (pb, hb) = place_of(need[j]), place_of(need[j + 1])
                s1[h, k, j // 2] = jnp.where(lower, moved(sums[pa], ha, 0), moved(sums[pb], hb, 1))
        on(lambda k: copy1(h, k).start(), ks)

    def add_sums(h, sums, ks):
        on(lambda k: landed1(h, k).wait_recv(), ks)
        for k in ks:
            d, need = NEIGHBOURS[k], shared(NEIGHBOURS[k ^ 1])
            for j, b in enumerate(need):
                p, target = place_of((b[0] + d[0], b[1] + d[1]))
                value = moved(r1[h, k, j // 2], j % 2, target)
                sums[p] = sums[p] + jnp.where(lower == (target == 0), value, 0.0)
        return sums

    def relay(h):
        sums = add_sums(h, [part[h, p] for p in range(PAIRS - 1)] + [blank], (2, 3))
        own = part[h, PAIRS - 1]
        for p in range(PAIRS):
            part[h, p] = sums[p]
        send_sums(h, sums[:-1] + [sums[-1] + own], (0, 1))

    @pl.loop(0, HALVES)
    def _(h):
        rows(3, functools.partial(tangent_row, h, 3, t3, t4, A3, R3))
        mine = []
        for p in range(PAIRS):
            mine.append(acc[h, p] + read(h, p, [(t4, 4, *at) for at in touched(p, 3)]))
            part[h, p] = mine[p]
        send_sums(h, mine, (2, 3))

    not_first = jnp.where(lane1 == 0, 0.0, 1.0)
    not_last = jnp.where(lane1 == layers - 1, 0.0, 1.0)

    def prior(h):
        for x in range(sx):
            X = x + lo_x
            mid = [vp[h, x + 1, y + 1] for y in range(sy)]
            for y in range(sy):
                Y = y + lo_y
                v = mid[y]
                near = [vp[h, i + 1, y + 1] for i in (x - 1, x + 1) if 0 <= i < sx]
                near += [mid[j] for j in (y - 1, y + 1) if 0 <= j < sy]
                beside = add(near) + not_first * up(v) + not_last * down(v)
                first_sensors = coef(R0, X, Y) * (coef(N1, X, Y) * t1[h, X, Y])
                result[h, x * sy + y] = (
                    PRIOR_WEIGHT * ((6.0 + PRIOR_SHIFT) * v - beside) - first_sensors
                )

    for h in range(HALVES):
        prior(h)
        if h == HALVES - 1:
            for p in range(PAIRS):
                for t in range(2, STEPS + 1):
                    for X, Y in touched(p, t - 1):
                        mark = jnp.broadcast_to(marks[t - 2, X, pl.ds(Y, 1), :], (depth, layers))
                        marked[t - 2, X, Y] = mark.astype(jnp.bfloat16)
        relay(h)


    def inject(p, t, reach, use):
        wanted = touched(p, reach)
        for start in range(0, len(wanted), chunk):
            some = wanted[start:start + chunk]
            high, low = [], []
            for X, Y in some:
                mark = marked[t - 2, X, Y]
                high.append(ysplit[p, 0] * mark)
                low.append(ysplit[p, 1] * mark)
            left = jnp.concatenate([jnp.concatenate(high, axis=0), jnp.concatenate(low, axis=0)], axis=1)
            got = lax.dot_general(left, zi[p], (((1,), (1,)), ((), ())), preferred_element_type=jnp.float32)
            for i, (X, Y) in enumerate(some):
                use(X, Y, got[i * depth:(i + 1) * depth])

    def adjoint(hold, q, ka, X, Y, centre):
        a = hold[X, Y] if centre is None else centre
        return (
            coef(ka, X, Y) * a
            + ((q[X - 1, Y] + q[X + 1, Y]) + (q[X, Y - 1] + q[X, Y + 1]))
            + coef(DL, X, Y) * up(a)
            + coef(DC, X, Y) * down(a)
        )

    def adjoint_row(h, reach, hold, q, new_hold, new_q, placed, tangent, ka, kn, X, ex, inward):
        for Y in range(lo_y - reach + ex, hi_y + reach - ex):
            a = adjoint(hold, q, ka, X, Y, None) + placed[X, Y]
            if ex == 0 and out_y(Y) == 0:
                a = a + coef(kn, X, Y) * tangent[h, X, Y]
            new_hold[X, Y] = a
            new_q[X, Y] = dcoef(X, Y) * a

    inner = [
        (X, Y) for X in range(lo_x, hi_x) for Y in range(lo_y, hi_y) if (X, Y) not in touched(PAIRS - 1, 3)
    ]

    @pl.loop(0, HALVES)
    def _(h):
        total = add_sums(h, [part[h, p] for p in range(PAIRS)], (0, 1))
        for p in range(PAIRS):
            top = total[p].astype(jnp.bfloat16)
            ysplit[p, 0] = top
            ysplit[p, 1] = (total[p] - top.astype(jnp.float32)).astype(jnp.bfloat16)

        def last_step(X, Y, value):
            a4[X, Y] = value
            q4[X, Y] = dcoef(X, Y) * value

        def last_own(X, Y, value):
            last_step(X, Y, value + coef(N4, X, Y) * t4[h, X, Y])

        def to_three(X, Y, value):
            pl3[X, Y] = value

        def to_two(X, Y, value):
            pl2[X, Y] = value

        for p in range(PAIRS):
            inject(p, 4, 3, last_own if p == PAIRS - 1 else last_step)
            inject(p, 3, 2, to_three)
            inject(p, 2, 1, to_two)
        for X, Y in inner:
            last_step(X, Y, coef(N4, X, Y) * t4[h, X, Y])
        rows(2, functools.partial(adjoint_row, h, 2, a4, q4, a3, q3, pl3, t3, A3, N3))
        rows(1, functools.partial(adjoint_row, h, 1, a3, q3, a2, q2, pl2, t2, A2, N2))
        on(lambda k: landed_v(h, k).wait_recv(), sides)

        for x in range(sx):
            X = x + lo_x
            for y in range(sy):
                Y = y + lo_y
                middle = a2[X, Y]
                gradient = (
                    coef(R3, X, Y) * a4[X, Y] + coef(R2, X, Y) * a3[X, Y] + coef(R1, X, Y) * middle
                    + coef(R0, X, Y) * adjoint(a2, q2, A1, X, Y, middle)
                )
                outside = [vp[h, i, y + 1] for i in (0, sx + 1) if abs(i - x - 1) == 1]
                outside += [vp[h, x + 1, j] for j in (0, sy + 1) if abs(j - y - 1) == 1]
                if outside:
                    gradient = gradient + PRIOR_WEIGHT * add(outside)
                at = x * sy + y
                result[h, at] = result[h, at] - gradient
                pltpu.make_async_copy(
                    result.at[h, at], out.at[pl.ds(h * depth, depth), at], out_sem.at[h]
                ).start()

    for h in range(HALVES):
        pltpu.make_async_copy(result.at[h], result.at[h], out_sem.at[h]).wait()
    on(lambda k: copy0(k).wait_send(), every)
    on(lambda k: copy3(k).wait_send(), every)
    for h in range(HALVES):
        on(lambda k: copy_v(h, k).wait_send(), sides)
        on(lambda k: copy1(h, k).wait_send(), sides)


def on_device(conc_start, diffusion, courant, uptake, directions, sensor_cell, sensor_step):
    count_dir, sx, sy, layers = directions.shape
    depth = count_dir // HALVES
    sensors = sensor_cell.shape[-1]
    assert sensors <= layers // 2 and min(sx, sy) >= 2 * REACH and depth % 16 == 0
    ex_n, ey_n = sx + 2 * REACH, pl.cdiv(sy + 2 * REACH, TILE) * TILE
    vmem = pltpu.VMEM
    wide = sy + 2 * REACH
    both = vmem((HALVES, ex_n, wide, depth, layers), jnp.float32)
    one = vmem((ex_n, wide, depth, layers), jnp.float32)

    def table(n):
        return vmem((n, ex_n, ey_n, layers), jnp.float32)

    tiles = 1 + sum(WIDTHS)
    sems = pltpu.SemaphoreType.DMA
    result = pl.pallas_call(
        functools.partial(kernel, sx, sy, depth),
        out_shape=jax.ShapeDtypeStruct((count_dir, sx * sy, layers), jnp.float32),
        in_specs=[pl.BlockSpec(memory_space=pltpu.HBM)] * 7,
        out_specs=pl.BlockSpec(memory_space=pl.ANY),
        scratch_shapes=[
            *[vmem((sx, sy, layers), jnp.float32)] * 4,
            vmem((count_dir * sx * sy, layers), jnp.float32),
            *[vmem((1, sensors), jnp.int32)] * 2,
            vmem((HALVES, sx * sy, depth, layers), jnp.float32),
            vmem((STEPS - 1, ex_n, wide, depth, layers), jnp.bfloat16),
            vmem((HALVES, sx + 2, sy + 2, depth, layers), jnp.float32),
            *[both] * 4,
            *[one] * 8,
            table(7),
            table(15),
            table(STEPS - 1),
            vmem((sx, ey_n, layers), jnp.float32),
            vmem((TILE, layers), jnp.int32),
            vmem((PAIRS, 2 * layers, layers), jnp.bfloat16),
            vmem((PAIRS, layers, 2 * layers), jnp.bfloat16),
            vmem((HALVES, PAIRS, depth, layers), jnp.float32),
            vmem((HALVES, PAIRS, depth, layers), jnp.float32),
            vmem((PAIRS, 2, depth, layers), jnp.bfloat16),
            vmem((8, tiles, TILE, layers), jnp.float32),
            vmem((8, tiles, TILE, layers), jnp.float32),
            vmem((8, 2, TILE, layers), jnp.float32),
            vmem((8, 2, TILE, layers), jnp.float32),
            vmem((HALVES, 4, 3, depth, layers), jnp.float32),
            vmem((HALVES, 4, 3, depth, layers), jnp.float32),
            sems((7,)), sems((HALVES,)),
            sems((8,)), sems((8,)),
            sems((8,)), sems((8,)),
            sems((HALVES, 4)), sems((HALVES, 4)),
            sems((HALVES, 4)), sems((HALVES, 4)),
        ],
        compiler_params=pltpu.CompilerParams(
            collective_id=0, has_side_effects=True, vmem_limit_bytes=56 * 2**20
        ),
    )(
        conc_start, diffusion, courant, uptake,
        directions.reshape(count_dir * sx * sy, layers),
        sensor_cell.reshape(1, sensors), sensor_step.reshape(1, sensors),
    )
    return result.reshape(count_dir, sx, sy, layers)


def solution(mesh):
    in_specs = (
        P("gx", "gy", None),
        P("gx", "gy", None),
        P("gx", "gy", None),
        P("gx", "gy", None),
        P(None, "gx", "gy", None),
        P("gx", "gy", None),
        P("gx", "gy", None),
    )
    out_specs = P(None, "gx", "gy", None)
    return jax.shard_map(
        on_device, mesh=mesh, in_specs=in_specs, out_specs=out_specs, check_vma=False
    )
```
